32 devices in a mesh: rep: 2 (over x), exp: 16 (over z, y, core).
Axes of the slice: x: 2, y: 2, z: 4, core: 2. Of those that a mesh axis runs over, the one named last changes fastest.
Arguments:
- tokens: bfloat16 [2, 2048, 2048], P('rep', 'exp'), may hold values from -6 to 6
- cotangent: bfloat16 [2, 2048, 2048], P('rep', 'exp'), may hold values from -6 to 6
- routes: int32 [2, 2048, 8], P('rep', 'exp'), may hold values from 0 to 15, all different within a row; in each aligned block of 128 rows (0 to 127, 128 to 255, ..., all dimensions but the last counted through in order) at most 96 rows name the same one
- router_pair_weight: bfloat16 [2, 2048, 8], P('rep', 'exp'), may hold values from 0.019897461 to 0.5
- capacity: int32 [16], replicated, may hold values from 512 to 1024, as said below
- training_step_index: int32 [1], replicated, may hold values from 0 to 999
- frozen_gate_matrix: bfloat16 [16, 2048, 768], P('exp'), may hold values from -0.125 to 0.125
- frozen_up_matrix: bfloat16 [16, 2048, 768], P('exp'), may hold values from -0.125 to 0.125
- frozen_down_matrix: bfloat16 [16, 768, 2048], P('exp'), may hold values from -0.21875 to 0.21875
- adapter_input_factor: float32 [2, 16, 16, 768], P('rep', 'exp'), may hold values from -0.6 to 0.6
- adapter_output_factor: float32 [2, 16, 16, 2048], P('rep', 'exp'), may hold values from -1.5 to 1.5
- input_first_moment: float32 [2, 16, 16, 768], P('rep', 'exp'), may hold values from -2 to 2
- output_first_moment: float32 [2, 16, 16, 2048], P('rep', 'exp'), may hold values from -2 to 2
- input_second_moment: float32 [2, 16, 16, 768], P('rep', 'exp'), may hold values from 0.05 to 5
- output_second_moment: float32 [2, 16, 16, 2048], P('rep', 'exp'), may hold values from 0.05 to 5
Outputs:
- combined: bfloat16 [2, 2048, 2048], P('rep', 'exp')
- new_lora_in: float32 [2, 16, 16, 768], P('rep', 'exp')
- new_lora_out: float32 [2, 16, 16, 2048], P('rep', 'exp')
- new_first_in: float32 [2, 16, 16, 768], P('rep', 'exp')
- new_first_out: float32 [2, 16, 16, 2048], P('rep', 'exp')
- new_second_in: float32 [2, 16, 16, 768], P('rep', 'exp')
- new_second_out: float32 [2, 16, 16, 2048], P('rep', 'exp')
The draws below stay inside these ranges and needn't reach their ends.
Inputs may be any that keep to these rules, and one draw needn't show every extreme that they name: `routes`: in the rows of one device, no expert is named more than 96 times; a token names distinct experts. The largest capacity is exactly 1024.
All inputs are finite; a program needn't handle non-finite values.
Results may differ from the reference program's by a relative error of at most 0.007.
Values may be sent and summed in bfloat16 or wider, within the bound.
A program may use at most 128 MiB of HBM per device.

```python
import math
import jax
import jax.numpy as jnp
import numpy as np
from jax import lax

HIDDEN_WIDTH = 2048
EXPERT_UNITS = 768
ADAPTER_RANK = 16
TOP = 8
TOK_DEV = 128
REPLICA_COUNT = 2
TOKENS = 2048
WINDOW_EXPERTS = 16
MOST = 96
CAP_MOST = 1024
N_REP = 2


def draw_capacity(key, part):
    first_key, second_key = jax.random.split(jax.random.fold_in(key, 17))
    drawn = jax.random.randint(first_key, (WINDOW_EXPERTS,), CAP_MOST // 2, CAP_MOST + 1)
    chosen = jax.random.randint(second_key, (), 0, WINDOW_EXPERTS)
    return jnp.where(jnp.arange(WINDOW_EXPERTS) == chosen, CAP_MOST, drawn).astype(jnp.int32)


def block_scale(rng, dims, cuts, least, largest):
    factor_of, own = 1.0, jax.random.fold_in(rng, 6)
    for axis_at, parts in cuts:
        steps = jnp.exp(jax.random.uniform(jax.random.fold_in(own, axis_at), (parts,), jnp.float32, least / len(cuts), largest / len(cuts)))
        factor_of = factor_of * jnp.repeat(steps, dims[axis_at] // parts).reshape([-1 if axis == axis_at else 1 for axis in range(len(dims))])
    return factor_of


def routed_block(rng, own, number, rows, count, top, bound, lean):
    sequence = jax.random.permutation(rng, count)
    crowded, ordinary = load_shares(count, rows * top, bound, lean, True), load_shares(count, rows * top, bound, lean, False)
    places = jnp.arange(count)

    def named(tallies, rotation):
        used = int((tallies > 0).sum())
        fixed = max(1, used // 4)
        shifted = fixed + (places - fixed + rotation * (used - fixed)) % max(1, count - fixed)
        return jnp.zeros((count,), jnp.int32).at[sequence[jnp.where(places < fixed, places, shifted)]].set(jnp.asarray(tallies, jnp.int32))

    tallies = jnp.where(number % 4 == 0, named(crowded, number // 4), named(ordinary, number - number // 4 - 1))
    mixed = jax.random.permutation(jax.random.fold_in(own, 3), count)
    giver, receiver = mixed[0:count // 2 * 2:2], mixed[1:count // 2 * 2:2]
    slack = jnp.minimum(tallies[giver] - 1, bound - tallies[receiver]) // 2
    slack = jnp.where((giver == sequence[0]) | (receiver == sequence[0]) | (tallies[receiver] == 0), 0, jnp.maximum(slack, 0))
    shifted = jax.random.randint(jax.random.fold_in(own, 4), (count // 2,), 0, 1 << 20) % (slack + 1)
    tallies = tallies.at[giver].add(-shifted).at[receiver].add(shifted)
    labels = jnp.searchsorted(jnp.cumsum(tallies), jnp.arange(rows * top), side="right").astype(jnp.int32)
    grid = labels.reshape(top, rows).T
    grid = grid[jax.random.permutation(jax.random.fold_in(own, 1), rows)]
    rotation = jax.random.randint(jax.random.fold_in(own, 2), (rows, 1), 0, top)
    return jnp.take_along_axis(grid, (jnp.arange(top)[None, :] + rotation) % top, axis=1)


def load_shares(number_of, total, reach, skew, full):
    portions = [(1 << 20) // math.isqrt(grade ** skew) + 1 for grade in range(1, number_of + 1)]
    largest = reach if full else min(reach, max(-(-total // number_of), total * portions[0] // sum(portions)))
    least = 1 if total - largest >= number_of - 1 else 0
    holding, surplus = [largest] + [least] * (number_of - 1), total - largest - least * (number_of - 1)
    while surplus > 0:
        free = [i for i in range(1, number_of) if holding[i] < largest] or [i for i in range(1, number_of) if holding[i] < reach]
        pool, left = sum([portions[i] for i in free]), surplus
        for i in free:
            more = min(reach - holding[i], max(1, left * portions[i] // pool), surplus)
            holding[i] = holding[i] + more
            surplus = surplus - more
    return np.array(holding)


def noise(rng, dims, width, reach, cuts=(), kind=jnp.bfloat16):
    result = width * jax.random.normal(rng, dims, jnp.float32)
    if cuts:
        result = result * block_scale(rng, dims, cuts, -0.22, 0.18)
    return jnp.clip(result, -reach, reach).astype(kind)


def setup_inputs(seed: int = 0) -> dict:
    arg_keys = jax.random.split(jax.random.key(seed), 16)
    tokens = noise(arg_keys[0], (REPLICA_COUNT, TOKENS, HIDDEN_WIDTH), 1.0, 6.0, ((0, 2), (1, 16)))
    cotangent = noise(arg_keys[1], (REPLICA_COUNT, TOKENS, HIDDEN_WIDTH), 1.0, 6.0, ((0, 2), (1, 16)))
    routes_keys = jax.random.split(jax.random.fold_in(arg_keys[2], 1), REPLICA_COUNT * TOKENS // TOK_DEV)
    routes_turns = jax.random.permutation(jax.random.fold_in(arg_keys[2], 3), REPLICA_COUNT * TOKENS // TOK_DEV)
    routes = jax.vmap(lambda own, number: routed_block(jax.random.fold_in(arg_keys[2], 2), own, number, TOK_DEV, WINDOW_EXPERTS, TOP, MOST, 2))(routes_keys, routes_turns).reshape((REPLICA_COUNT, TOKENS, TOP))
    router_pair_weight = jnp.clip(jnp.exp(math.log(0.5) - 3.224016 * jax.random.uniform(arg_keys[3], (REPLICA_COUNT, TOKENS, TOP), jnp.float32) ** block_scale(arg_keys[3], (REPLICA_COUNT, TOKENS, TOP), ((0, 2), (1, 16)), -0.2, 0.2)), 0.019897461, 0.5).astype(jnp.bfloat16)
    capacity = draw_capacity(jax.random.fold_in(arg_keys[15], 71), 0)
    training_step_index = jax.random.randint(arg_keys[5], (1,), 0, 1000).astype(jnp.int32)
    frozen_gate_matrix = noise(arg_keys[6], (WINDOW_EXPERTS, HIDDEN_WIDTH, EXPERT_UNITS), HIDDEN_WIDTH ** -0.5, 0.125, ((0, 16),))
    frozen_up_matrix = noise(arg_keys[7], (WINDOW_EXPERTS, HIDDEN_WIDTH, EXPERT_UNITS), HIDDEN_WIDTH ** -0.5, 0.125, ((0, 16),))
    frozen_down_matrix = noise(arg_keys[8], (WINDOW_EXPERTS, EXPERT_UNITS, HIDDEN_WIDTH), EXPERT_UNITS ** -0.5, 0.21875, ((0, 16),))
    adapter_input_factor = noise(arg_keys[9], (REPLICA_COUNT, WINDOW_EXPERTS, ADAPTER_RANK, EXPERT_UNITS), 0.1, 0.6, ((0, 2), (1, 16)), jnp.float32)
    adapter_output_factor = noise(arg_keys[10], (REPLICA_COUNT, WINDOW_EXPERTS, ADAPTER_RANK, HIDDEN_WIDTH), 0.25, 1.5, ((0, 2), (1, 16)), jnp.float32)
    input_first_moment = noise(arg_keys[11], (REPLICA_COUNT, WINDOW_EXPERTS, ADAPTER_RANK, EXPERT_UNITS), 0.3, 2.0, ((0, 2), (1, 16)), jnp.float32)
    output_first_moment = noise(arg_keys[12], (REPLICA_COUNT, WINDOW_EXPERTS, ADAPTER_RANK, HIDDEN_WIDTH), 0.3, 2.0, ((0, 2), (1, 16)), jnp.float32)
    input_second_moment = jnp.clip(jnp.exp(math.log(5.0) - 4.6051702 * jax.random.uniform(arg_keys[13], (REPLICA_COUNT, WINDOW_EXPERTS, ADAPTER_RANK, EXPERT_UNITS), jnp.float32) ** block_scale(arg_keys[13], (REPLICA_COUNT, WINDOW_EXPERTS, ADAPTER_RANK, EXPERT_UNITS), ((0, 2), (1, 16)), -0.2, 0.2)), 0.05, 5.0)
    output_second_moment = jnp.clip(jnp.exp(math.log(5.0) - 4.6051702 * jax.random.uniform(arg_keys[14], (REPLICA_COUNT, WINDOW_EXPERTS, ADAPTER_RANK, HIDDEN_WIDTH), jnp.float32) ** block_scale(arg_keys[14], (REPLICA_COUNT, WINDOW_EXPERTS, ADAPTER_RANK, HIDDEN_WIDTH), ((0, 2), (1, 16)), -0.2, 0.2)), 0.05, 5.0)
    return dict(tokens=tokens, cotangent=cotangent, routes=routes, router_pair_weight=router_pair_weight, capacity=capacity, training_step_index=training_step_index, frozen_gate_matrix=frozen_gate_matrix, frozen_up_matrix=frozen_up_matrix, frozen_down_matrix=frozen_down_matrix, adapter_input_factor=adapter_input_factor, adapter_output_factor=adapter_output_factor, input_first_moment=input_first_moment, output_first_moment=output_first_moment, input_second_moment=input_second_moment, output_second_moment=output_second_moment)


adapter_scale = 0.5
beta_one = 0.9
beta_two = 0.999
learn_rate = 0.02
weight_decay = 0.01
epsilon = 1e-08

def route_ranks(route_rows):
    expert_ids = jnp.arange(WINDOW_EXPERTS, dtype=jnp.int32)
    route_hits = (route_rows[:, :, None] == expert_ids[None, None, :]).astype(jnp.int32)
    per_token = lax.optimization_barrier(jnp.sum(route_hits, axis=1))
    before = jnp.cumsum(per_token, axis=0) - per_token
    return (route_hits, lax.optimization_barrier(jnp.sum(route_hits * before[:, None, :], axis=2)))

def one_replica(item, capacity, frozen_gate_matrix, frozen_up_matrix, frozen_down_matrix):
    token_rows, cot_rows, route_rows, weight_rows, in_rep, out_rep = item
    route_hits, rank_table = route_ranks(route_rows)
    cap_pairs = lax.optimization_barrier(jnp.sum(route_hits * capacity[None, None, :], axis=2))
    kept_mask = rank_table < cap_pairs
    total_slots = WINDOW_EXPERTS * CAP_MOST
    place = jnp.where(kept_mask, route_rows * CAP_MOST + rank_table, total_slots).reshape(-1)
    token_ids = jnp.broadcast_to(jnp.arange(TOKENS, dtype=jnp.int32)[:, None], (TOKENS, TOP)).reshape(-1)
    row_index = jnp.zeros((total_slots,), jnp.int32).at[place].set(token_ids, mode='drop')
    row_valid = jnp.zeros((total_slots,), jnp.float32).at[place].set(1.0, mode='drop')
    row_weight = jnp.zeros((total_slots,), jnp.float32).at[place].set(weight_rows.astype(jnp.float32).reshape(-1), mode='drop')
    input_factor_batch = in_rep.astype(jnp.bfloat16)
    output_factor_batch = out_rep.astype(jnp.bfloat16)

    def one_expert(expert_item):
        slot_index, slot_valid, slot_weight, w_gate, w_up, down_projection_matrix, in_one, single_output_rows = expert_item
        picked = token_rows[slot_index] * slot_valid[:, None].astype(jnp.bfloat16)
        row_gradient_values = (slot_weight[:, None] * cot_rows[slot_index].astype(jnp.float32)).astype(jnp.bfloat16)
        gate = jnp.dot(picked, w_gate, preferred_element_type=jnp.float32)
        upper = jnp.dot(picked, w_up, preferred_element_type=jnp.float32)
        hidden_activation = (jax.nn.silu(gate) * upper).astype(jnp.bfloat16)
        projected_rank_rows = jnp.dot(hidden_activation, in_one.T, preferred_element_type=jnp.float32).astype(jnp.bfloat16)
        expert_result_rows = (jnp.dot(hidden_activation, down_projection_matrix, preferred_element_type=jnp.float32) + adapter_scale * jnp.dot(projected_rank_rows, single_output_rows, preferred_element_type=jnp.float32)).astype(jnp.bfloat16)
        output_factor_gradient = adapter_scale * jnp.dot(projected_rank_rows.T, row_gradient_values, preferred_element_type=jnp.float32)
        returned_rank_rows = jnp.dot(row_gradient_values, single_output_rows.T, preferred_element_type=jnp.float32).astype(jnp.bfloat16)
        input_factor_gradient = adapter_scale * jnp.dot(returned_rank_rows.T, hidden_activation, preferred_element_type=jnp.float32)
        return (expert_result_rows, input_factor_gradient, output_factor_gradient)
    expert_result_rows, input_factor_gradient, output_factor_gradient = lax.map(one_expert, (row_index.reshape(WINDOW_EXPERTS, CAP_MOST), row_valid.reshape(WINDOW_EXPERTS, CAP_MOST), row_weight.reshape(WINDOW_EXPERTS, CAP_MOST), frozen_gate_matrix, frozen_up_matrix, frozen_down_matrix, input_factor_batch, output_factor_batch))
    out_table = expert_result_rows.reshape(total_slots, HIDDEN_WIDTH)
    pick_index = jnp.where(kept_mask, route_rows * CAP_MOST + rank_table, 0)
    summed = jnp.zeros((TOKENS, HIDDEN_WIDTH), jnp.float32)
    for slot_k in range(TOP):
        scale_k = jnp.where(kept_mask[:, slot_k], weight_rows[:, slot_k].astype(jnp.float32), jnp.float32(0.0))
        summed = summed + scale_k[:, None] * out_table[pick_index[:, slot_k]].astype(jnp.float32)
    return (summed.astype(jnp.bfloat16), input_factor_gradient, output_factor_gradient)

def adam_update(averaged, gradient, first_moment, second_moment, fix_one, fix_two):
    new_first = beta_one * first_moment + (1.0 - beta_one) * gradient
    new_second = beta_two * second_moment + (1.0 - beta_two) * gradient * gradient
    stepped = new_first / fix_one / (jnp.sqrt(new_second / fix_two) + epsilon)
    return (averaged - learn_rate * (stepped + weight_decay * averaged), new_first, new_second)

def reference(tokens, cotangent, routes, router_pair_weight, capacity, training_step_index, frozen_gate_matrix, frozen_up_matrix, frozen_down_matrix, adapter_input_factor, adapter_output_factor, input_first_moment, output_first_moment, input_second_moment, output_second_moment):

    def replica_function(item):
        return one_replica(item, capacity, frozen_gate_matrix, frozen_up_matrix, frozen_down_matrix)
    combined, input_factor_gradient, output_factor_gradient = lax.map(replica_function, (tokens, cotangent, routes, router_pair_weight, adapter_input_factor, adapter_output_factor))
    levels = N_REP.bit_length() - 1
    level_bit = (training_step_index[0] % levels).astype(jnp.int32)
    gossip_neighbor = jnp.bitwise_xor(jnp.arange(REPLICA_COUNT, dtype=jnp.int32), jnp.left_shift(jnp.ones((), jnp.int32), level_bit))
    mean_input_factor = 0.5 * (adapter_input_factor + adapter_input_factor[gossip_neighbor])
    mean_output_factor = 0.5 * (adapter_output_factor + adapter_output_factor[gossip_neighbor])
    power = (training_step_index[0] + 1).astype(jnp.float32)
    fix_one = 1.0 - jnp.power(jnp.float32(beta_one), power)
    fix_two = 1.0 - jnp.power(jnp.float32(beta_two), power)
    new_in, new_first_in, new_second_in = adam_update(mean_input_factor, input_factor_gradient, input_first_moment, input_second_moment, fix_one, fix_two)
    new_out, new_first_out, new_second_out = adam_update(mean_output_factor, output_factor_gradient, output_first_moment, output_second_moment, fix_one, fix_two)
    return (combined, new_in, new_out, new_first_in, new_first_out, new_second_in, new_second_out)
```

```python
from functools import partial

import jax
import jax.numpy as jnp
from jax import lax
from jax.experimental import pallas as pl
from jax.experimental.pallas import tpu as pltpu
from jax.sharding import PartitionSpec as P

adapter_scale = 0.5
beta_one = 0.9
beta_two = 0.999
learn_rate = 0.02
weight_decay = 0.01
epsilon = 1e-08
MESH = pl.DeviceIdType.MESH
SIDE_OUT = 32
SIDE_BACK = 48


def layer_kernel(
    levels,
    cap_ref,
    routes_ref,
    weight_ref,
    in_ref,
    out_ref,
    x_hbm,
    cot_hbm,
    gate_hbm,
    up_hbm,
    down_hbm,
    comb_ref,
    gin_ref,
    gout_ref,
    near_in_ref,
    near_out_ref,
    rows,
    part,
    from_core,
    from_y,
    from_ys,
    cm_lo,
    cm_hi,
    cs_lo,
    cs_hi,
    hid,
    gate_w,
    up_w,
    down_w,
    cots,
    in_b,
    outs,
    tables,
    kept,
    mine,
    mine_t,
    low_mine,
    low_got,
    back_mine,
    back_got,
    grad_mine,
    grad_got,
    near_in,
    near_out,
    main_s,
    main_r,
    side_s,
    side_r,
    ob_s,
    ob_r,
    tile_s,
    tile_r,
    core_s,
    core_r,
    ym_s,
    ym_r,
    ys_s,
    ys_r,
    cm_s,
    cmu_r,
    cmd_r,
    cs_s,
    csu_r,
    csd_r,
    tab_s,
    tab_r,
    low_s,
    low_r,
    back_s,
    back_r,
    grad_s,
    grad_r,
    cot_s,
    cot_r,
    near_s,
    near_r,
    load_s,
):
    n = 16
    depth = 4
    pairs = n // 2
    f32 = jnp.float32
    bf16 = jnp.bfloat16
    me = lax.axis_index("exp")
    rep = lax.axis_index("rep")
    z, y, c = me // 4, (me // 2) % 2, me % 2
    home = me // 2
    tok = rows.shape[2]
    rank = in_ref.shape[0]
    cut_f = tok - SIDE_OUT
    cut_c = tok - SIDE_BACK
    core_mate = me + 1 - 2 * c
    y_mate = me + 2 - 4 * y
    inner = (z > 0) & (z < depth - 1)
    outer = (z == 0) | (z == depth - 1)
    skip = jnp.where(inner, 1, 0)

    def copy(src, dst, send, recv, device, axis="exp"):
        return pltpu.make_async_remote_copy(
            src_ref=src,
            dst_ref=dst,
            send_sem=send,
            recv_sem=recv,
            device_id={axis: device},
            device_id_type=MESH,
        )

    def order(s):
        table = ((0, 1, 2, 3), (1, 2, 0, 3), (2, 1, 3, 0), (3, 2, 1, 0))
        value = s * 0
        for row in range(depth):
            for col in range(depth):
                value = jnp.where((z == row) & (s == col), table[row][col], value)
        return value

    def main_to(kind, zz, device):
        block = rows.at[zz * 2 + y, c, 0:cut_f]
        return copy(block, block, main_s.at[kind, zz], main_r.at[zz * 2 + y], device)

    def main_in(p):
        block = rows.at[p, c, 0:cut_f]
        return copy(block, block, main_s.at[2, 0], main_r.at[p], y_mate)

    def side_to(kind, p, device):
        block = rows.at[p, c, cut_f:tok]
        return copy(block, block, side_s.at[kind, p], side_r.at[p], device)

    def ob_to(kind, zz, device):
        block = outs.at[zz * 2 + y]
        return copy(block, block, ob_s.at[kind, zz], ob_r.at[zz * 2 + y], device)

    def ob_in(p):
        return copy(outs.at[p], outs.at[p], ob_s.at[2, 0], ob_r.at[p], y_mate)

    def tile_to(p):
        return copy(rows.at[p, c], rows.at[p, c], tile_s.at[p], tile_r.at[p], core_mate)

    def tile_in(p):
        return copy(rows.at[p, 1 - c], rows.at[p, 1 - c], tile_s.at[p], tile_r.at[p], core_mate)

    def core_to(p):
        return copy(part.at[p, 1 - c], from_core.at[p], core_s.at[p], core_r.at[p], core_mate)

    def ym_to(zt):
        return copy(
            part.at[zt * 2 + 1 - y, c, 0:cut_c], from_y.at[zt], ym_s.at[zt], ym_r.at[zt], y_mate
        )

    def ys_to():
        return copy(
            part.at[z * 2 + 1 - y, c, cut_c:tok], from_ys, ys_s.at[0], ys_r.at[0], y_mate
        )

    def cm_up(zt):
        return copy(
            part.at[zt * 2 + y, c, 0:cut_c], cm_lo.at[zt], cm_s.at[zt], cmu_r.at[zt], me + 4
        )

    def cm_down(zt):
        return copy(
            part.at[zt * 2 + y, c, 0:cut_c], cm_hi.at[zt], cm_s.at[zt], cmd_r.at[zt], me - 4
        )

    def cs_up(p):
        return copy(part.at[p, c, cut_c:tok], cs_lo.at[p], cs_s.at[p], csu_r.at[p], me + 4)

    def cs_down(p):
        return copy(part.at[p, c, cut_c:tok], cs_hi.at[p], cs_s.at[p], csd_r.at[p], me - 4)

    def send_table(d):
        return copy(tables.at[me], tables.at[me], tab_s.at[d], tab_r.at[me], lax.rem(me + d, n))

    def send_low(p):
        return copy(low_mine.at[p], low_got.at[home], low_s.at[p], low_r.at[home], p * 2 + c)

    def send_back(p):
        return copy(back_mine.at[p], back_got.at[home], back_s.at[p], back_r.at[home], p * 2 + c)

    def send_grad(p):
        return copy(grad_mine.at[p], grad_got.at[home], grad_s.at[p], grad_r.at[home], p * 2 + c)

    def send_cot():
        return copy(cots.at[c], cots.at[c], cot_s.at[0], cot_r.at[0], core_mate)

    def rep_mate(level):
        stride = 2**level
        return rep + stride * (1 - 2 * ((rep // stride) % 2))

    def send_near(level):
        return (
            copy(in_b, near_in.at[level], near_s.at[0, level], near_r.at[0, level], rep_mate(level), "rep"),
            copy(
                outs.at[home],
                near_out.at[level],
                near_s.at[1, level],
                near_r.at[1, level],
                rep_mate(level),
                "rep",
            ),
        )

    barrier = pltpu.get_barrier_semaphore()

    @pl.loop(1, n)
    def _(d):
        pl.semaphore_signal(
            barrier, inc=1, device_id={"exp": lax.rem(me + d, n)}, device_id_type=MESH
        )

    for level in range(levels):
        pl.semaphore_signal(
            barrier, inc=1, device_id={"rep": rep_mate(level)}, device_id_type=MESH
        )

    loads = [
        pltpu.make_async_copy(x_hbm, rows.at[home, c], load_s.at[0]),
        pltpu.make_async_copy(cot_hbm, cots.at[c], load_s.at[1]),
        pltpu.make_async_copy(gate_hbm, gate_w, load_s.at[2]),
        pltpu.make_async_copy(up_hbm, up_w, load_s.at[3]),
        pltpu.make_async_copy(down_hbm, down_w, load_s.at[4]),
    ]
    for load in loads:
        load.start()

    in_b[...] = in_ref[...].astype(bf16)
    outs[home] = out_ref[...].astype(bf16)
    expert = lax.broadcasted_iota(jnp.int32, (n, tok), 0)
    routed = routes_ref[...]
    weights = weight_ref[...].astype(f32)
    table = jnp.zeros((n, tok), f32)
    for k in range(routes_ref.shape[0]):
        table = table + jnp.where(routed[k : k + 1] == expert, weights[k : k + 1], 0.0)
    tables[me] = table.astype(bf16)

    pl.semaphore_wait(barrier, n - 1 + levels)
    loads[0].wait()

    def spread(zz, make, act):
        @pl.when((zz <= z) & (z < depth - 1))
        def _():
            act(make(0, me + 4))

        @pl.when((zz >= z) & (z > 0))
        def _():
            act(make(1, me - 4))

    def start(one):
        one.start()

    @pl.loop(1, n)
    def _(d):
        send_table(d).start()

    side_to(2, home, y_mate).start()
    spread(z, lambda kind, device: main_to(kind, z, device), start)
    main_to(2, z, y_mate).start()
    tile_to(home).start()
    spread(z, lambda kind, device: side_to(kind, home, device), start)
    side_to(2, z * 2 + 1 - y, y_mate).wait_recv()
    spread(z, lambda kind, device: side_to(kind, z * 2 + 1 - y, device), start)
    spread(z, lambda kind, device: ob_to(kind, z, device), start)
    ob_to(2, z, y_mate).start()
    for level in range(levels):
        for one in send_near(level):
            one.start()
    loads[1].wait()
    send_cot().start()

    @pl.loop(1, n)
    def _(d):
        source = lax.rem(me + d, n)
        copy(
            tables.at[source], tables.at[source], tab_s.at[d], tab_r.at[source], source
        ).wait_recv()

    later = lax.broadcasted_iota(jnp.int32, (tok, tok), 1)
    sooner = lax.broadcasted_iota(jnp.int32, (tok, tok), 0)
    strictly = (sooner < later).astype(bf16)
    which_expert = lax.broadcasted_iota(jnp.int32, (n, 1), 0)
    cap = jnp.zeros((n, 1), f32)
    for e in range(n):
        cap = jnp.where(which_expert == e, cap_ref[e].astype(f32), cap)
    all_weights = tables[...].astype(f32).reshape(n * n, tok)
    hits = (all_weights > 0).astype(f32)
    within = jnp.dot(hits.astype(bf16), strictly, preferred_element_type=f32)
    counts = jnp.sum(hits, axis=1, keepdims=True)
    before = jnp.zeros((n, 1), f32)
    for source in range(n):
        part_of = slice(source * n, (source + 1) * n)
        keep = before + within[part_of] < cap
        row = jnp.where(keep, all_weights[part_of], 0.0)
        kept[source] = row
        mine[source : source + 1, :] = jnp.sum(
            jnp.where(expert == me, row, 0.0), axis=0, keepdims=True
        )
        before = before + counts[part_of]
    mine_t[...] = mine[...].T
    lane = lax.broadcasted_iota(jnp.int32, (tok, n), 1)

    def transposed_dot(a, b):
        return lax.dot_general(a, b, (((1,), (1,)), ((), ())), preferred_element_type=f32)

    for load in loads[2:]:
        load.wait()

    def expert_pair(p):
        x = rows[p].reshape(2 * tok, rows.shape[3])
        gate = jnp.dot(x, gate_w[...], preferred_element_type=f32)
        upper = jnp.dot(x, up_w[...], preferred_element_type=f32)
        hidden = (gate / (1.0 + jnp.exp(-gate)) * upper).astype(bf16)
        hid[p] = hidden
        low_t = transposed_dot(in_b[...], hidden).astype(bf16).astype(f32)
        low = transposed_dot(hidden, in_b[...]).astype(bf16)
        result = jnp.dot(hidden, down_w[...], preferred_element_type=f32)
        result = result + adapter_scale * jnp.dot(low, outs[home], preferred_element_type=f32)
        for k in range(2):
            scale = jnp.sum(jnp.where(lane == p * 2 + k, mine_t[...], 0.0), axis=1, keepdims=True)
            part[p, k] = (scale * result[k * tok : (k + 1) * tok]).astype(bf16)
        weighted = jnp.concatenate(
            [low_t[:, k * tok : (k + 1) * tok] * mine[pl.ds(p * 2 + k, 1), :] for k in range(2)],
            axis=1,
        ).astype(bf16)

        @pl.when(p == home)
        def _():
            low_got[p] = weighted

        @pl.when(p != home)
        def _():
            low_mine[p] = weighted
            send_low(p).start()

        core_to(p).start()

    def finish_core(p):
        core_to(p).wait_recv()
        part[p, c] = (part[p, c].astype(f32) + from_core[p].astype(f32)).astype(bf16)

    def forward_main(zz):
        main_in(zz * 2 + y).wait_recv()
        spread(zz, lambda kind, device: main_to(kind, zz, device), start)
        main_to(2, zz, y_mate).start()

    def side_in(p):
        block = rows.at[p, c, cut_f:tok]
        copy(block, block, side_s.at[2, p], side_r.at[p], y_mate).wait_recv()

    def forward_side(zz):
        side_in(zz * 2 + y)
        spread(zz, lambda kind, device: side_to(kind, zz * 2 + y, device), start)
        tile_to(zz * 2 + y).start()
        side_in(zz * 2 + 1 - y)
        spread(zz, lambda kind, device: side_to(kind, zz * 2 + 1 - y, device), start)
        ob_in(zz * 2 + y).wait_recv()
        spread(zz, lambda kind, device: ob_to(kind, zz, device), start)
        ob_to(2, zz, y_mate).start()

    def side_chain(p):
        zt = p // 2

        @pl.when(inner & (zt > z))
        def _():
            cs_up(p).wait_recv()
            part[p, c, cut_c:tok] = (
                part[p, c, cut_c:tok].astype(f32) + cs_lo[p].astype(f32)
            ).astype(bf16)

        @pl.when(inner & (zt < z))
        def _():
            cs_down(p).wait_recv()
            part[p, c, cut_c:tok] = (
                part[p, c, cut_c:tok].astype(f32) + cs_hi[p].astype(f32)
            ).astype(bf16)

        @pl.when(zt > z)
        def _():
            cs_up(p).start()

        @pl.when(zt < z)
        def _():
            cs_down(p).start()

    def main_chain(zt):
        p = zt * 2 + y
        ym_to(zt).wait_recv()

        @pl.when(outer)
        def _():
            part[p, c, 0:cut_c] = (
                part[p, c, 0:cut_c].astype(f32) + from_y[zt].astype(f32)
            ).astype(bf16)

        @pl.when(inner & (zt > z))
        def _():
            cm_up(zt).wait_recv()
            part[p, c, 0:cut_c] = (
                part[p, c, 0:cut_c].astype(f32) + from_y[zt].astype(f32) + cm_lo[zt].astype(f32)
            ).astype(bf16)

        @pl.when(inner & (zt < z))
        def _():
            cm_down(zt).wait_recv()
            part[p, c, 0:cut_c] = (
                part[p, c, 0:cut_c].astype(f32) + from_y[zt].astype(f32) + cm_hi[zt].astype(f32)
            ).astype(bf16)

        @pl.when(zt > z)
        def _():
            cm_up(zt).start()

        @pl.when(zt < z)
        def _():
            cm_down(zt).start()

    @pl.loop(0, depth + 1)
    def _(s):
        now = order(s)
        last = order(s - 1)
        older = order(s - 2)
        ahead = s + skip
        new = order(ahead)
        forwards = (s > 0) & (ahead < depth)

        @pl.when((s == 1) & inner)
        def _():
            forward_main(now)

        @pl.when(forwards)
        def _():
            forward_main(new)

        @pl.when(s > 0)
        def _():
            main_in(last * 2 + 1 - y).wait_recv()
            tile_to(last * 2 + 1 - y).start()

        @pl.when((s == 1) & inner)
        def _():
            forward_side(now)

        @pl.loop(0, 2)
        def _(which):
            zt = jnp.where(which == 0, last, now)
            yt = jnp.where(which == 0, 1 - y, y)

            @pl.when((s + which > 0) & (s + which < depth + 1))
            def _():
                tile_in(zt * 2 + yt).wait_recv()
                expert_pair(zt * 2 + yt)

            @pl.when((which == 0) & forwards)
            def _():
                forward_side(new)

            @pl.when((which == 0) & (s >= 2) & outer)
            def _():
                @pl.when(older != z)
                def _():
                    main_chain(older)

            @pl.when((s + which > 0) & (s + which < depth + 1))
            def _():
                finish_core(zt * 2 + yt)

                @pl.when((which == 0) & (zt != z))
                def _():
                    ym_to(zt).start()

                @pl.when(outer & (zt != z))
                def _():
                    side_chain(zt * 2 + yt)

    ym_to(z).start()

    @pl.loop(0, depth)
    def _(zz):
        ob_in(zz * 2 + 1 - y).wait_recv()

    send_cot_in = copy(cots.at[1 - c], cots.at[1 - c], cot_s.at[0], cot_r.at[0], core_mate)
    send_cot_in.wait_recv()
    both = cots[...].reshape(2 * tok, cots.shape[2])
    returned = transposed_dot(outs[...].reshape(pairs * rank, cots.shape[2]), both)
    for p in range(pairs):
        weight = jnp.concatenate(
            [kept[home * 2 + k, pl.ds(p * 2 + c, 1), :] for k in range(2)], axis=1
        )
        back = (returned[p * rank : (p + 1) * rank] * weight).astype(bf16)

        @pl.when(home == p)
        def _():
            back_got[p] = back

        @pl.when(home != p)
        def _():
            back_mine[p] = back
            send_back(p).start()

    def relay(item):
        up_first = ((2, 3, 0), (3, 0, 3))[0]
        first = jnp.where(item == 0, up_first[0], jnp.where(item == 1, up_first[1], up_first[2]))
        return jnp.where(z == 1, first, 3 - first)

    def relay_step(item):
        zt = relay(item)
        side_chain(zt * 2 + y)
        side_chain(zt * 2 + 1 - y)
        main_chain(zt)

    @pl.when(inner)
    def _():
        relay_step(0)

    @pl.loop(0, pairs)
    def _(p):
        @pl.when(p != home)
        def _():
            copy(low_mine.at[p], low_got.at[p], low_s.at[p], low_r.at[p], p * 2 + c).wait_recv()

    grads = adapter_scale * jnp.dot(
        low_got[...].reshape(pairs * rank, 2 * tok),
        cots[...].reshape(2 * tok, cots.shape[2]),
        preferred_element_type=f32,
    )
    grad_mine[...] = grads.astype(bf16).reshape(grad_mine.shape)

    @pl.loop(0, pairs)
    def _(p):
        @pl.when(p == home)
        def _():
            grad_got[p] = grad_mine[p]

        @pl.when(p != home)
        def _():
            send_grad(p).start()

    @pl.when(outer)
    def _():
        main_chain(depth - 1 - z)

    @pl.when(inner)
    def _():
        @pl.loop(1, depth - 1)
        def _(item):
            relay_step(item)

    gin_ref[...] = jnp.zeros_like(gin_ref)

    @pl.loop(0, pairs)
    def _(p):
        @pl.when(p != home)
        def _():
            copy(
                back_mine.at[p], back_got.at[p], back_s.at[p], back_r.at[p], p * 2 + c
            ).wait_recv()

        gin_ref[...] += adapter_scale * jnp.dot(back_got[p], hid[p], preferred_element_type=f32)

    def with_side(p):
        value = part[p, c, cut_c:tok].astype(f32)

        @pl.when(z > 0)
        def _():
            cs_up(p).wait_recv()

        @pl.when(z < depth - 1)
        def _():
            cs_down(p).wait_recv()

        low = jnp.where(z > 0, cs_lo[p].astype(f32), 0.0)
        high = jnp.where(z < depth - 1, cs_hi[p].astype(f32), 0.0)
        return value + low + high

    @pl.when(z == 0)
    def _():
        cm_lo[z] = jnp.zeros_like(cm_lo[z])
        cs_lo[z * 2] = jnp.zeros_like(cs_lo[z * 2])
        cs_lo[z * 2 + 1] = jnp.zeros_like(cs_lo[z * 2])

    @pl.when(z == depth - 1)
    def _():
        cm_hi[z] = jnp.zeros_like(cm_hi[z])
        cs_hi[z * 2] = jnp.zeros_like(cs_hi[z * 2])
        cs_hi[z * 2 + 1] = jnp.zeros_like(cs_hi[z * 2])

    part[z * 2 + 1 - y, c, cut_c:tok] = with_side(z * 2 + 1 - y).astype(bf16)
    ys_to().start()

    ym_to(z).wait_recv()

    @pl.when(z > 0)
    def _():
        cm_up(z).wait_recv()

    @pl.when(z < depth - 1)
    def _():
        cm_down(z).wait_recv()

    comb_ref[0:cut_c] = (
        part[home, c, 0:cut_c].astype(f32)
        + from_y[z].astype(f32)
        + cm_lo[z].astype(f32)
        + cm_hi[z].astype(f32)
    ).astype(bf16)
    own_side = with_side(home)

    gout_ref[...] = jnp.zeros_like(gout_ref)

    @pl.loop(0, pairs)
    def _(p):
        @pl.when(p != home)
        def _():
            copy(
                grad_mine.at[p], grad_got.at[p], grad_s.at[p], grad_r.at[p], p * 2 + c
            ).wait_recv()

        gout_ref[...] += grad_got[p].astype(f32)

    for level in range(levels):
        for one in send_near(level):
            one.wait_recv()
    near_in_ref[...] = near_in[...]
    near_out_ref[...] = near_out[...]
    ys_to().wait_recv()
    comb_ref[cut_c:tok] = (own_side + from_ys[...].astype(f32)).astype(bf16)

    def sent(one):
        one.wait_send()

    @pl.loop(0, depth)
    def _(zz):
        spread(zz, lambda kind, device: main_to(kind, zz, device), sent)
        main_to(2, zz, y_mate).wait_send()
        spread(zz, lambda kind, device: side_to(kind, zz * 2, device), sent)
        spread(zz, lambda kind, device: side_to(kind, zz * 2 + 1, device), sent)
        spread(zz, lambda kind, device: ob_to(kind, zz, device), sent)
        ob_to(2, zz, y_mate).wait_send()
        ym_to(zz).wait_send()

        @pl.when(zz != z)
        def _():
            copy(part.at[0, 0, 0:cut_c], cm_lo.at[0], cm_s.at[zz], cmu_r.at[zz], y_mate).wait_send()

    side_to(2, home, y_mate).wait_send()
    ys_to().wait_send()
    send_cot().wait_send()

    @pl.loop(0, pairs)
    def _(p):
        tile_to(p).wait_send()
        core_to(p).wait_send()

        @pl.when(p // 2 != z)
        def _():
            copy(part.at[0, 0, cut_c:tok], cs_lo.at[0], cs_s.at[p], csu_r.at[p], y_mate).wait_send()

        @pl.when(p != home)
        def _():
            send_low(p).wait_send()
            send_back(p).wait_send()
            send_grad(p).wait_send()

    @pl.loop(1, n)
    def _(d):
        send_table(d).wait_send()

    for level in range(levels):
        for one in send_near(level):
            one.wait_send()


def layer(levels, cap, routes, weights, in_f, out_f, x, cot, gate, up, down):
    n = cap.shape[0]
    tok, width = cot.shape
    rank, units = in_f.shape
    pairs, depth = n // 2, n // 4
    vmem = pl.BlockSpec(memory_space=pltpu.VMEM)
    hbm = pl.BlockSpec(memory_space=pl.ANY)
    bf16 = jnp.bfloat16
    f32 = jnp.float32
    dma = pltpu.SemaphoreType.DMA
    main, side = tok - SIDE_BACK, SIDE_BACK
    return pl.pallas_call(
        partial(layer_kernel, levels),
        out_shape=(
            jax.ShapeDtypeStruct((tok, width), bf16),
            jax.ShapeDtypeStruct((rank, units), f32),
            jax.ShapeDtypeStruct((rank, width), f32),
            jax.ShapeDtypeStruct((levels, rank, units), bf16),
            jax.ShapeDtypeStruct((levels, rank, width), bf16),
        ),
        in_specs=[pl.BlockSpec(memory_space=pltpu.SMEM)] + [vmem] * 4 + [hbm] * 5,
        out_specs=(vmem,) * 5,
        scratch_shapes=[
            pltpu.VMEM((pairs, 2, tok, width), bf16),
            pltpu.VMEM((pairs, 2, tok, width), bf16),
            pltpu.VMEM((pairs, tok, width), bf16),
            pltpu.VMEM((depth, main, width), bf16),
            pltpu.VMEM((side, width), bf16),
            pltpu.VMEM((depth, main, width), bf16),
            pltpu.VMEM((depth, main, width), bf16),
            pltpu.VMEM((pairs, side, width), bf16),
            pltpu.VMEM((pairs, side, width), bf16),
            pltpu.VMEM((pairs, 2 * tok, units), bf16),
            pltpu.VMEM((width, units), bf16),
            pltpu.VMEM((width, units), bf16),
            pltpu.VMEM((units, width), bf16),
            pltpu.VMEM((2, tok, width), bf16),
            pltpu.VMEM((rank, units), bf16),
            pltpu.VMEM((pairs, rank, width), bf16),
            pltpu.VMEM((n, n, tok), bf16),
            pltpu.VMEM((n, n, tok), f32),
            pltpu.VMEM((n, tok), f32),
            pltpu.VMEM((tok, n), f32),
            pltpu.VMEM((pairs, rank, 2 * tok), bf16),
            pltpu.VMEM((pairs, rank, 2 * tok), bf16),
            pltpu.VMEM((pairs, rank, 2 * tok), bf16),
            pltpu.VMEM((pairs, rank, 2 * tok), bf16),
            pltpu.VMEM((pairs, rank, width), bf16),
            pltpu.VMEM((pairs, rank, width), bf16),
            pltpu.VMEM((levels, rank, units), bf16),
            pltpu.VMEM((levels, rank, width), bf16),
            dma((3, depth)),
            dma((pairs,)),
            dma((3, pairs)),
            dma((pairs,)),
            dma((3, depth)),
            dma((pairs,)),
            dma((pairs,)),
            dma((pairs,)),
            dma((pairs,)),
            dma((pairs,)),
            dma((depth,)),
            dma((depth,)),
            dma((1,)),
            dma((1,)),
            dma((depth,)),
            dma((depth,)),
            dma((depth,)),
            dma((pairs,)),
            dma((pairs,)),
            dma((pairs,)),
            dma((n,)),
            dma((n,)),
            dma((pairs,)),
            dma((pairs,)),
            dma((pairs,)),
            dma((pairs,)),
            dma((pairs,)),
            dma((pairs,)),
            dma((1,)),
            dma((1,)),
            dma((2, levels)),
            dma((2, levels)),
            dma((5,)),
        ],
        compiler_params=pltpu.CompilerParams(
            collective_id=0, has_side_effects=True, vmem_limit_bytes=62 * 1024 * 1024
        ),
        cost_estimate=pl.CostEstimate(
            flops=20_000_000_000, bytes_accessed=30_000_000, transcendentals=0
        ),
    )(cap, routes, weights, in_f, out_f, x, cot, gate, up, down)


def adam_kernel(levels, level_ref, fix_one_ref, fix_two_ref, comb, *refs):
    comb_out = refs[10]
    comb_out[...] = comb[...]
    fix_one, fix_two = fix_one_ref[0], fix_two_ref[0]
    for side in range(2):
        own, near, grad, first, second = refs[side * 5 : side * 5 + 5]
        new, new_first_ref, new_second_ref = refs[11 + side], refs[13 + side], refs[15 + side]
        other = near[0].astype(jnp.float32)
        for level in range(1, levels):
            other = jnp.where(level_ref[0] == level, near[level].astype(jnp.float32), other)
        averaged = 0.5 * (own[...] + other)
        gradient = grad[...]
        new_first = beta_one * first[...] + (1.0 - beta_one) * gradient
        new_second = beta_two * second[...] + (1.0 - beta_two) * gradient * gradient
        stepped = new_first / fix_one / (jnp.sqrt(new_second / fix_two) + epsilon)
        new[...] = averaged - learn_rate * (stepped + weight_decay * averaged)
        new_first_ref[...] = new_first
        new_second_ref[...] = new_second


def adam(levels, level, fix_one, fix_two, comb, *arrays):
    vmem = pl.BlockSpec(memory_space=pltpu.VMEM)
    smem = pl.BlockSpec(memory_space=pltpu.SMEM)
    own_in, own_out = arrays[0], arrays[5]
    f_in = jax.ShapeDtypeStruct(own_in.shape, jnp.float32)
    f_out = jax.ShapeDtypeStruct(own_out.shape, jnp.float32)
    return pl.pallas_call(
        partial(adam_kernel, levels),
        out_shape=(jax.ShapeDtypeStruct(comb.shape, comb.dtype), f_in, f_out, f_in, f_out, f_in, f_out),
        in_specs=[smem] * 3 + [vmem] * 11,
        out_specs=(vmem,) * 7,
        compiler_params=pltpu.CompilerParams(vmem_limit_bytes=16 * 1024 * 1024),
    )(level, fix_one, fix_two, comb, *arrays)


def per_device(
    tokens,
    cotangent,
    routes,
    router_pair_weight,
    capacity,
    training_step_index,
    frozen_gate_matrix,
    frozen_up_matrix,
    frozen_down_matrix,
    adapter_input_factor,
    adapter_output_factor,
    input_first_moment,
    output_first_moment,
    input_second_moment,
    output_second_moment,
):
    devices = lax.axis_size("exp")
    assert frozen_gate_matrix.shape[0] == 1 and devices == 16
    levels = lax.axis_size("rep").bit_length() - 1
    combined, grad_in, grad_out, near_in, near_out = layer(
        levels,
        capacity,
        routes[0].T,
        router_pair_weight[0].T,
        adapter_input_factor[0, 0],
        adapter_output_factor[0, 0],
        tokens[0],
        cotangent[0],
        frozen_gate_matrix[0],
        frozen_up_matrix[0],
        frozen_down_matrix[0],
    )
    level = training_step_index % levels
    power = (training_step_index + 1).astype(jnp.float32)
    fix_one = 1.0 - jnp.power(jnp.float32(beta_one), power)
    fix_two = 1.0 - jnp.power(jnp.float32(beta_two), power)
    results = adam(
        levels,
        level,
        fix_one,
        fix_two,
        combined,
        adapter_input_factor[0, 0],
        near_in,
        grad_in,
        input_first_moment[0, 0],
        input_second_moment[0, 0],
        adapter_output_factor[0, 0],
        near_out,
        grad_out,
        output_first_moment[0, 0],
        output_second_moment[0, 0],
    )
    return (results[0][None],) + tuple(one[None, None] for one in results[1:])


def solution(mesh):
    placed = (
        P("rep", "exp", None),
        P("rep", "exp", None),
        P("rep", "exp", None),
        P("rep", "exp", None),
        P(),
        P(),
        P("exp", None, None),
        P("exp", None, None),
        P("exp", None, None),
        P("rep", "exp", None, None),
        P("rep", "exp", None, None),
        P("rep", "exp", None, None),
        P("rep", "exp", None, None),
        P("rep", "exp", None, None),
        P("rep", "exp", None, None),
    )
    return jax.shard_map(
        per_device,
        mesh=mesh,
        in_specs=placed,
        out_specs=(
            P("rep", "exp", None),
            P("rep", "exp", None, None),
            P("rep", "exp", None, None),
            P("rep", "exp", None, None),
            P("rep", "exp", None, None),
            P("rep", "exp", None, None),
            P("rep", "exp", None, None),
        ),
        check_vma=False,
    )
```

```python
from functools import partial

import jax
import jax.numpy as jnp
from jax import lax
from jax.experimental import pallas as pl
from jax.experimental.pallas import tpu as pltpu
from jax.sharding import PartitionSpec as P

adapter_scale = 0.5
beta_one = 0.9
beta_two = 0.999
learn_rate = 0.02
weight_decay = 0.01
epsilon = 1e-08
MESH = pl.DeviceIdType.MESH
SIDE_OUT = 16
BACK_OUTER = 32
BACK_INNER = 32
PARTS_OUT = 2
PARTS_BACK = 2
OUTER = (
    "own", "kept", "fsx0", "fob0", "pair00", "fs1", "fy10", "fy11", "fy20", "pair10", "fs2",
    "post10", "fsx1", "fy21", "cs10", "fm11", "ty1", "fsx2", "pair20", "fobx0", "pair11", "fy31",
    "ty2", "post20", "g11", "pair21", "fy30", "fm10", "cs20", "fs3", "ty0", "post21", "cs21",
    "fsx3", "ym20", "pair30", "post11", "cs11", "ty3", "post30", "cs30", "ym21", "pair31", "g12",
    "fob3", "post31", "cs31", "post00", "fm20", "ym31", "g13", "ym30", "pair01", "fm30", "ym10",
    "cm31", "post01", "cm20", "g10", "cm30", "fm21", "ym00", "fob1", "ym11", "g2", "fob2", "back",
    "cm21", "fm31", "gout", "ys", "cm10", "cm11", "gin", "ym01", "fin2", "fin1",
)
INNER = (
    "own", "fy00", "kept", "fsx1", "fm20", "fm01", "fy01", "fy20", "fm00", "fs0", "ty1", "fsx0",
    "fm21", "fs2", "pair11", "pair20", "fsx2", "ty0", "fy21", "fm31", "pair00", "pair01", "fy30",
    "fs3", "fm30", "ty2", "fsx3", "post01", "fy31", "fob0", "fob1", "pair21", "fob3", "pair30",
    "ym00", "g12", "ty3", "post21", "fobx1", "pair31", "cs21", "g13", "post31", "post30", "ym31",
    "post20", "cs30", "ym20", "g10", "cs31", "ym01", "ym21", "fob2", "ym30", "post11", "back",
    "pair10", "post00", "cs01", "cm31", "ys", "cs00", "g11", "g2", "ym10", "cm20", "cm30",
    "post10", "ym11", "cs20", "cm01", "gin", "cm21", "cm00", "gout", "fin2", "fin1",
)


def cut_rows(rows, count, first=0):
    units = rows // 16
    ranges = []
    for one in range(count):
        size = 16 * (units // count + (1 if one < units % count else 0))
        ranges.append((first, first + size))
        first += size
    return ranges


def layer_kernel(
    levels,
    cap_ref,
    routes_ref,
    weight_ref,
    in_ref,
    out_ref,
    x_hbm,
    cot_hbm,
    gate_hbm,
    up_hbm,
    down_hbm,
    comb_ref,
    gin_ref,
    gout_ref,
    near_in_ref,
    near_out_ref,
    rows,
    part,
    from_core,
    from_y,
    from_ys,
    cm_in,
    cs_in,
    hid,
    gate_w,
    up_w,
    down_w,
    cots,
    in_b,
    outs,
    tables,
    kept,
    mine,
    mine_t,
    low_mine,
    low_got,
    back_mine,
    back_got,
    grad_mine,
    grad_got,
    grad_y,
    grad_yin,
    near_in,
    near_out,
    main_s,
    main_r,
    side_s,
    side_r,
    ob_s,
    ob_r,
    tile_s,
    tile_r,
    core_s,
    core_r,
    ym_s,
    ym_r,
    ys_s,
    ys_r,
    cm_s,
    cm_r,
    cs_s,
    cs_r,
    tab_s,
    tab_r,
    low_s,
    low_r,
    back_s,
    back_r,
    grad_s,
    grad_r,
    gy_s,
    gy_r,
    cot_s,
    cot_r,
    near_s,
    near_r,
    load_s,
):
    n = 16
    depth = 4
    pairs = n // 2
    f32 = jnp.float32
    bf16 = jnp.bfloat16
    me = lax.axis_index("exp")
    rep = lax.axis_index("rep")
    z, y, c = me // 4, (me // 2) % 2, me % 2
    home = me // 2
    tok = rows.shape[2]
    width = rows.shape[3]
    rank = in_ref.shape[0]
    cut_f = tok - SIDE_OUT
    out_parts = cut_rows(cut_f, PARTS_OUT)
    core_mate = me + 1 - 2 * c
    y_mate = me + 2 - 4 * y
    turned = z // 2
    sign = 1 - 2 * turned
    roles = ((z == 0) | (z == depth - 1), (z > 0) & (z < depth - 1))

    def real(zz):
        return 3 * turned + sign * zz

    def pair_of(zz, col):
        return real(zz) * 2 + (y if col == 0 else 1 - y)

    def cut_c(zz):
        return tok - (BACK_OUTER if zz in (0, depth - 1) else BACK_INNER)

    def back_parts(zz):
        return cut_rows(cut_c(zz), PARTS_BACK)

    def copy(src, dst, send, recv, device, axis="exp"):
        return pltpu.make_async_remote_copy(
            src_ref=src,
            dst_ref=dst,
            send_sem=send,
            recv_sem=recv,
            device_id={axis: device},
            device_id_type=MESH,
        )

    def towards(kind):
        return (me + 4 * sign, me - 4 * sign, y_mate)[kind]

    def moving(kind):
        return turned if kind == 0 else 1 - turned

    def main_to(kind, zz, part_at):
        lo, hi = out_parts[part_at]
        p = pair_of(zz, 0)
        block = rows.at[p, c, lo:hi]
        return copy(block, block, main_s.at[kind, zz, part_at], main_r.at[p, part_at], towards(kind))

    def main_in(zz, col, part_at):
        lo, hi = out_parts[part_at]
        p = pair_of(zz, col)
        block = rows.at[p, c, lo:hi]
        return copy(block, block, main_s.at[2, zz, part_at], main_r.at[p, part_at], y_mate)

    def side_to(kind, zz, col):
        p = pair_of(zz, col)
        block = rows.at[p, c, cut_f:tok]
        return copy(block, block, side_s.at[kind, zz * 2 + col], side_r.at[p], towards(kind))

    def ob_to(kind, zz, col):
        p = pair_of(zz, col)
        return copy(outs.at[p], outs.at[p], ob_s.at[kind, zz * 2 + col], ob_r.at[p], towards(kind))

    def tile_to(p):
        return copy(rows.at[p, c], rows.at[p, c], tile_s.at[p], tile_r.at[p], core_mate)

    def tile_in(p):
        return copy(rows.at[p, 1 - c], rows.at[p, 1 - c], tile_s.at[p], tile_r.at[p], core_mate)

    def core_to(p):
        return copy(part.at[p, 1 - c], from_core.at[p], core_s.at[p], core_r.at[p], core_mate)

    def ym_to(zz, part_at):
        lo, hi = back_parts(zz)[part_at]
        zt = real(zz)
        return copy(
            part.at[pair_of(zz, 1), c, lo:hi],
            from_y.at[zt, lo:hi],
            ym_s.at[zt, part_at],
            ym_r.at[zt, part_at],
            y_mate,
        )

    def ys_to(zz):
        size = tok - cut_c(zz)
        return copy(
            part.at[pair_of(zz, 1), c, cut_c(zz) : tok],
            from_ys.at[0:size],
            ys_s.at[0],
            ys_r.at[0],
            y_mate,
        )

    def cm_to(kind, zz, part_at):
        lo, hi = back_parts(zz)[part_at]
        zt = real(zz)
        return copy(
            part.at[pair_of(zz, 0), c, lo:hi],
            cm_in.at[moving(kind), zt, lo:hi],
            cm_s.at[zt, part_at],
            cm_r.at[moving(kind), zt, part_at],
            towards(kind),
        )

    def cs_to(kind, zz, col):
        p = pair_of(zz, col)
        size = tok - cut_c(zz)
        return copy(
            part.at[p, c, cut_c(zz) : tok],
            cs_in.at[moving(kind), p, 0:size],
            cs_s.at[p],
            cs_r.at[moving(kind), p],
            towards(kind),
        )

    def send_table(d):
        return copy(tables.at[me], tables.at[me], tab_s.at[d], tab_r.at[me], lax.rem(me + d, n))

    def send_low(p):
        return copy(low_mine.at[p], low_got.at[home], low_s.at[p], low_r.at[home], p * 2 + c)

    def send_back(p):
        return copy(back_mine.at[p], back_got.at[home], back_s.at[p], back_r.at[home], p * 2 + c)

    def send_grad(zz):
        zt = real(zz)
        return copy(grad_mine.at[zt], grad_got.at[z], grad_s.at[zt], grad_r.at[z], me + 4 * (zt - z))

    def send_grad_y():
        return copy(grad_y, grad_yin, gy_s.at[0], gy_r.at[0], y_mate)

    def send_cot():
        return copy(cots.at[c], cots.at[c], cot_s.at[0], cot_r.at[0], core_mate)

    def rep_mate(level):
        stride = 2**level
        return rep + stride * (1 - 2 * ((rep // stride) % 2))

    def send_near(level):
        return (
            copy(in_b, near_in.at[level], near_s.at[0, level], near_r.at[0, level], rep_mate(level), "rep"),
            copy(
                outs.at[home],
                near_out.at[level],
                near_s.at[1, level],
                near_r.at[1, level],
                rep_mate(level),
                "rep",
            ),
        )

    barrier = pltpu.get_barrier_semaphore()

    @pl.loop(1, n)
    def _(d):
        pl.semaphore_signal(
            barrier, inc=1, device_id={"exp": lax.rem(me + d, n)}, device_id_type=MESH
        )

    for level in range(levels):
        pl.semaphore_signal(
            barrier, inc=1, device_id={"rep": rep_mate(level)}, device_id_type=MESH
        )

    loads = [
        pltpu.make_async_copy(x_hbm, rows.at[home, c], load_s.at[0]),
        pltpu.make_async_copy(cot_hbm, cots.at[c], load_s.at[1]),
        pltpu.make_async_copy(gate_hbm, gate_w, load_s.at[2]),
        pltpu.make_async_copy(up_hbm, up_w, load_s.at[3]),
        pltpu.make_async_copy(down_hbm, down_w, load_s.at[4]),
    ]
    for load in loads:
        load.start()

    in_b[...] = in_ref[...].astype(bf16)
    outs[home] = out_ref[...].astype(bf16)
    expert = lax.broadcasted_iota(jnp.int32, (n, tok), 0)
    routed = routes_ref[...]
    weights = weight_ref[...].astype(f32)
    table = jnp.zeros((n, tok), f32)
    for k in range(routes_ref.shape[0]):
        table = table + jnp.where(routed[k : k + 1] == expert, weights[k : k + 1], 0.0)
    tables[me] = table.astype(bf16)

    pl.semaphore_wait(barrier, n - 1 + levels)
    loads[0].wait()

    def transposed_dot(a, b):
        return lax.dot_general(a, b, (((1,), (1,)), ((), ())), preferred_element_type=f32)

    def find_kept():
        for level in range(levels):
            for one in send_near(level):
                one.start()
        loads[1].wait()
        send_cot().start()

        @pl.loop(1, n)
        def _(d):
            source = lax.rem(me + d, n)
            copy(
                tables.at[source], tables.at[source], tab_s.at[d], tab_r.at[source], source
            ).wait_recv()

        later = lax.broadcasted_iota(jnp.int32, (tok, tok), 1)
        sooner = lax.broadcasted_iota(jnp.int32, (tok, tok), 0)
        strictly = (sooner < later).astype(bf16)
        which_expert = lax.broadcasted_iota(jnp.int32, (n, 1), 0)
        cap = jnp.zeros((n, 1), f32)
        for e in range(n):
            cap = jnp.where(which_expert == e, cap_ref[e].astype(f32), cap)
        all_weights = tables[...].astype(f32).reshape(n * n, tok)
        hits = (all_weights > 0).astype(f32)
        within = jnp.dot(hits.astype(bf16), strictly, preferred_element_type=f32)
        counts = jnp.sum(hits, axis=1, keepdims=True)
        before = jnp.zeros((n, 1), f32)
        for source in range(n):
            part_of = slice(source * n, (source + 1) * n)
            keep = before + within[part_of] < cap
            row = jnp.where(keep, all_weights[part_of], 0.0)
            kept[source] = row
            mine[source : source + 1, :] = jnp.sum(
                jnp.where(expert == me, row, 0.0), axis=0, keepdims=True
            )
            before = before + counts[part_of]
        mine_t[...] = mine[...].T
        copy(cots.at[1 - c], cots.at[1 - c], cot_s.at[0], cot_r.at[0], core_mate).wait_recv()
        for load in loads[2:]:
            load.wait()

    lane = lax.broadcasted_iota(jnp.int32, (tok, n), 1)

    def expert_pair(p):
        x = rows[p].reshape(2 * tok, width)
        gate = jnp.dot(x, gate_w[...], preferred_element_type=f32)
        upper = jnp.dot(x, up_w[...], preferred_element_type=f32)
        hidden = (gate / (1.0 + jnp.exp(-gate)) * upper).astype(bf16)
        hid[p] = hidden
        low_t = transposed_dot(in_b[...], hidden).astype(bf16).astype(f32)
        low = transposed_dot(hidden, in_b[...]).astype(bf16)
        result = jnp.dot(hidden, down_w[...], preferred_element_type=f32)
        result = result + adapter_scale * jnp.dot(low, outs[home], preferred_element_type=f32)
        for k in range(2):
            scale = jnp.sum(jnp.where(lane == p * 2 + k, mine_t[...], 0.0), axis=1, keepdims=True)
            part[p, k] = (scale * result[k * tok : (k + 1) * tok]).astype(bf16)
        core_to(p).start()
        weighted = jnp.concatenate(
            [low_t[:, k * tok : (k + 1) * tok] * mine[pl.ds(p * 2 + k, 1), :] for k in range(2)],
            axis=1,
        ).astype(bf16)

        @pl.when(p == home)
        def _():
            low_got[p] = weighted

        @pl.when(p != home)
        def _():
            low_mine[p] = weighted
            send_low(p).start()

    started = ([], [])

    def send(role, make):
        make().start()
        started[role].append(make)

    def spread(role, zz, make):
        for kind, goes in ((0, zz <= role), (1, zz >= role and role > 0)):
            if goes:
                send(role, partial(make, kind))

    def sources(role):
        return ((1,), (0, 1))[role]

    def take(p, lo, hi, others):
        total = part[p, c, lo:hi].astype(f32)
        for one in others:
            total = total + one.astype(f32)
        return total

    def arrived(role, zz, h):
        if (zz, h) not in waited[role]:
            waited[role].append((zz, h))
            main_in(zz, 0, h).wait_recv()

    def step(role, name):
        word = name.rstrip("0123456789")
        digits = [int(one) for one in name[len(word) :]]
        zz = digits[0] if digits else role
        last = digits[1] if len(digits) > 1 else 0
        along = 0 if zz > role else 1
        if word == "own":

            @pl.loop(1, n)
            def _(d):
                send_table(d).start()

            send(role, lambda: side_to(2, role, 0))
            for h in range(PARTS_OUT):
                spread(role, role, lambda kind, h=h: main_to(kind, role, h))
                send(role, lambda h=h: main_to(2, role, h))
            spread(role, role, lambda kind: side_to(kind, role, 0))
            tile_to(home).start()
        elif word == "fob":
            if zz == role:
                send(role, lambda: ob_to(2, role, 0))
                spread(role, role, lambda kind: ob_to(kind, role, 0))
            else:
                for col in range(2):
                    ob_to(2, zz, col).wait_recv()
                for col in range(2):
                    spread(role, zz, lambda kind, col=col: ob_to(kind, zz, col))
        elif word == "fobx":
            ob_to(2, role, 1).wait_recv()
            spread(role, role, lambda kind: ob_to(kind, role, 1))
        elif word in ("fm", "fy"):
            arrived(role, zz, last)
            if word == "fm":
                spread(role, zz, lambda kind: main_to(kind, zz, last))
            else:
                send(role, lambda: main_to(2, zz, last))
        elif word == "fs":
            for h in range(PARTS_OUT):
                arrived(role, zz, h)
            side_to(2, zz, 0).wait_recv()
            spread(role, zz, lambda kind: side_to(kind, zz, 0))
            tile_to(pair_of(zz, 0)).start()
        elif word == "fsx":
            side_to(2, zz, 1).wait_recv()
            spread(role, zz, lambda kind: side_to(kind, zz, 1))
        elif word == "ty":
            for h in range(PARTS_OUT):
                main_in(zz, 1, h).wait_recv()
            tile_to(pair_of(zz, 1)).start()
        elif word == "post":
            p = pair_of(zz, last)
            core_to(p).wait_recv()
            part[p, c] = (part[p, c].astype(f32) + from_core[p].astype(f32)).astype(bf16)
        elif word == "ym":
            send(role, lambda: ym_to(zz, last))
        elif word == "cs":
            if role == 1:
                p = pair_of(zz, last)
                cs_to(along, zz, last).wait_recv()
                lo = cut_c(zz)
                total = take(p, lo, tok, [cs_in[moving(along), p, 0 : tok - lo]])
                part[p, c, lo:tok] = total.astype(bf16)
            send(role, lambda: cs_to(along, zz, last))
        elif word == "cm":
            p, zt = pair_of(zz, 0), real(zz)
            lo, hi = back_parts(zz)[last]
            ym_to(zz, last).wait_recv()
            others = [from_y[zt, lo:hi]]
            if role == 1:
                cm_to(along, zz, last).wait_recv()
                others.append(cm_in[moving(along), zt, lo:hi])
            part[p, c, lo:hi] = take(p, lo, hi, others).astype(bf16)
            send(role, lambda: cm_to(along, zz, last))
        elif word == "ys":
            p = pair_of(role, 1)
            lo = cut_c(role)
            for kind in sources(role):
                cs_to(kind, role, 1).wait_recv()
            others = [cs_in[moving(kind), p, 0 : tok - lo] for kind in sources(role)]
            part[p, c, lo:tok] = take(p, lo, tok, others).astype(bf16)
            send(role, lambda: ys_to(role))
        elif word == "fin":
            if name == "fin1":
                lo, hi = 0, cut_c(role)
                for h in range(PARTS_BACK):
                    ym_to(role, h).wait_recv()
                    for kind in sources(role):
                        cm_to(kind, role, h).wait_recv()
                others = [from_y[z, lo:hi]] + [cm_in[moving(k), z, lo:hi] for k in sources(role)]
            else:
                lo, hi = cut_c(role), tok
                ys_to(role).wait_recv()
                for kind in sources(role):
                    cs_to(kind, role, 0).wait_recv()
                others = [from_ys[0 : hi - lo]]
                others += [cs_in[moving(k), home, 0 : hi - lo] for k in sources(role)]
            comb_ref[lo:hi] = take(home, lo, hi, others).astype(bf16)
        elif word == "g":
            if name == "g2":
                for k in range(depth):
                    if k != role:
                        source = real(k)
                        copy(
                            grad_mine.at[source],
                            grad_got.at[source],
                            grad_s.at[source],
                            grad_r.at[source],
                            y_mate,
                        ).wait_recv()
                total = grad_got[0, 1 - y].astype(f32)
                for k in range(1, depth):
                    total = total + grad_got[k, 1 - y].astype(f32)
                grad_y[...] = total.astype(bf16)
                send(role, send_grad_y)
            else:
                zt = real(last)
                for col in range(2):
                    if last != role or col == 1:
                        p = pair_of(last, col)
                        copy(
                            low_mine.at[p], low_got.at[p], low_s.at[p], low_r.at[p], p * 2 + c
                        ).wait_recv()
                both = low_got[pl.ds(zt * 2, 2)].reshape(2 * rank, 2 * tok)
                grads = adapter_scale * jnp.dot(
                    both, cots[...].reshape(2 * tok, width), preferred_element_type=f32
                )
                grads = grads.astype(bf16).reshape(2, rank, width)
                if last == role:
                    grad_got[zt] = grads
                else:
                    grad_mine[zt] = grads
                    send(role, lambda: send_grad(last))
        elif word == "back":
            both = cots[...].reshape(2 * tok, width)
            returned = transposed_dot(outs[...].reshape(pairs * rank, width), both)
            for p in range(pairs):
                weight = jnp.concatenate(
                    [kept[home * 2 + k, pl.ds(p * 2 + c, 1), :] for k in range(2)], axis=1
                )
                back_mine[p] = (returned[p * rank : (p + 1) * rank] * weight).astype(bf16)

            back_got[home] = back_mine[home]

            @pl.loop(0, pairs)
            def _(p):
                @pl.when(p != home)
                def _():
                    send_back(p).start()

        elif word == "gin":
            gin_ref[...] = jnp.zeros_like(gin_ref)

            @pl.loop(0, pairs)
            def _(p):
                @pl.when(p != home)
                def _():
                    copy(
                        back_mine.at[p], back_got.at[p], back_s.at[p], back_r.at[p], p * 2 + c
                    ).wait_recv()

                gin_ref[...] += adapter_scale * jnp.dot(
                    back_got[p], hid[p], preferred_element_type=f32
                )

        elif word == "gout":
            send_grad_y().wait_recv()
            total = grad_yin[...].astype(f32)
            for k in range(depth):
                total = total + grad_got[k, y].astype(f32)
            gout_ref[...] = total
        else:
            raise ValueError(name)

    waited = ([], [])
    plans = (OUTER, INNER)
    begin = [plan.index("kept") for plan in plans]
    computes = [[one for one in plan if one.startswith("pair")] for plan in plans]

    def steps(role, names):
        for name in names:
            step(role, name)

    def between(role, k):
        plan = plans[role]
        lo = begin[role] if k == 0 else plan.index(computes[role][k - 1])
        hi = plan.index(computes[role][k]) if k < pairs else len(plan)
        return plan[lo + 1 : hi]

    for role in range(2):
        pl.when(roles[role])(partial(steps, role, plans[role][: begin[role]]))
    find_kept()

    @pl.loop(0, pairs)
    def _(i):
        for k in range(pairs):
            for role in range(2):
                pl.when(roles[role] & (i == k))(partial(steps, role, between(role, k)))
        p = i * 0
        for role in range(2):
            for k in range(pairs):
                zz, col = (int(one) for one in computes[role][k][-2:])
                p = jnp.where(roles[role] & (i == k), pair_of(zz, col), p)
        tile_in(p).wait_recv()
        expert_pair(p)

    for role in range(2):
        pl.when(roles[role])(partial(steps, role, between(role, pairs)))

    for level in range(levels):
        for one in send_near(level):
            one.wait_recv()
    near_in_ref[...] = near_in[...]
    near_out_ref[...] = near_out[...]

    def sent(role):
        for make in started[role]:
            make().wait_send()

    for role in range(2):
        pl.when(roles[role])(partial(sent, role))
    send_cot().wait_send()

    @pl.loop(0, pairs)
    def _(p):
        tile_to(p).wait_send()
        core_to(p).wait_send()

        @pl.when(p != home)
        def _():
            send_low(p).wait_send()
            send_back(p).wait_send()

    @pl.loop(1, n)
    def _(d):
        send_table(d).wait_send()

    for level in range(levels):
        for one in send_near(level):
            one.wait_send()


def layer(levels, cap, routes, weights, in_f, out_f, x, cot, gate, up, down):
    n = cap.shape[0]
    tok, width = cot.shape
    rank, units = in_f.shape
    pairs, depth = n // 2, n // 4
    vmem = pl.BlockSpec(memory_space=pltpu.VMEM)
    hbm = pl.BlockSpec(memory_space=pl.ANY)
    bf16 = jnp.bfloat16
    f32 = jnp.float32
    dma = pltpu.SemaphoreType.DMA
    main, side = tok - min(BACK_OUTER, BACK_INNER), max(BACK_OUTER, BACK_INNER)
    return pl.pallas_call(
        partial(layer_kernel, levels),
        out_shape=(
            jax.ShapeDtypeStruct((tok, width), bf16),
            jax.ShapeDtypeStruct((rank, units), f32),
            jax.ShapeDtypeStruct((rank, width), f32),
            jax.ShapeDtypeStruct((levels, rank, units), bf16),
            jax.ShapeDtypeStruct((levels, rank, width), bf16),
        ),
        in_specs=[pl.BlockSpec(memory_space=pltpu.SMEM)] + [vmem] * 4 + [hbm] * 5,
        out_specs=(vmem,) * 5,
        scratch_shapes=[
            pltpu.VMEM((pairs, 2, tok, width), bf16),
            pltpu.VMEM((pairs, 2, tok, width), bf16),
            pltpu.VMEM((pairs, tok, width), bf16),
            pltpu.VMEM((depth, main, width), bf16),
            pltpu.VMEM((side, width), bf16),
            pltpu.VMEM((2, depth, main, width), bf16),
            pltpu.VMEM((2, pairs, side, width), bf16),
            pltpu.VMEM((pairs, 2 * tok, units), bf16),
            pltpu.VMEM((width, units), bf16),
            pltpu.VMEM((width, units), bf16),
            pltpu.VMEM((units, width), bf16),
            pltpu.VMEM((2, tok, width), bf16),
            pltpu.VMEM((rank, units), bf16),
            pltpu.VMEM((pairs, rank, width), bf16),
            pltpu.VMEM((n, n, tok), bf16),
            pltpu.VMEM((n, n, tok), f32),
            pltpu.VMEM((n, tok), f32),
            pltpu.VMEM((tok, n), f32),
            pltpu.VMEM((pairs, rank, 2 * tok), bf16),
            pltpu.VMEM((pairs, rank, 2 * tok), bf16),
            pltpu.VMEM((pairs, rank, 2 * tok), bf16),
            pltpu.VMEM((pairs, rank, 2 * tok), bf16),
            pltpu.VMEM((depth, 2, rank, width), bf16),
            pltpu.VMEM((depth, 2, rank, width), bf16),
            pltpu.VMEM((rank, width), bf16),
            pltpu.VMEM((rank, width), bf16),
            pltpu.VMEM((levels, rank, units), bf16),
            pltpu.VMEM((levels, rank, width), bf16),
            dma((3, depth, PARTS_OUT)),
            dma((pairs, PARTS_OUT)),
            dma((3, pairs)),
            dma((pairs,)),
            dma((3, pairs)),
            dma((pairs,)),
            dma((pairs,)),
            dma((pairs,)),
            dma((pairs,)),
            dma((pairs,)),
            dma((depth, PARTS_BACK)),
            dma((depth, PARTS_BACK)),
            dma((1,)),
            dma((1,)),
            dma((depth, PARTS_BACK)),
            dma((2, depth, PARTS_BACK)),
            dma((pairs,)),
            dma((2, pairs)),
            dma((n,)),
            dma((n,)),
            dma((pairs,)),
            dma((pairs,)),
            dma((pairs,)),
            dma((pairs,)),
            dma((depth,)),
            dma((depth,)),
            dma((1,)),
            dma((1,)),
            dma((1,)),
            dma((1,)),
            dma((2, levels)),
            dma((2, levels)),
            dma((5,)),
        ],
        compiler_params=pltpu.CompilerParams(
            collective_id=0, has_side_effects=True, vmem_limit_bytes=62 * 1024 * 1024
        ),
        cost_estimate=pl.CostEstimate(
            flops=20_000_000_000, bytes_accessed=30_000_000, transcendentals=0
        ),
    )(cap, routes, weights, in_f, out_f, x, cot, gate, up, down)


def adam_kernel(levels, level_ref, fix_one_ref, fix_two_ref, *refs):
    comb, near_in, near_out, grad_in, grad_out = refs[:5]
    given, made, held, done = refs[5:11], refs[11:18], refs[18:22], refs[22]
    loads = [pltpu.make_async_copy(comb, made[0], done.at[4])]
    for k, (source, target) in enumerate(zip((near_in, near_out, grad_in, grad_out), held)):
        loads.append(pltpu.make_async_copy(source, target, done.at[k]))
    for load in loads:
        load.start()
    fix_one, fix_two = fix_one_ref[0], fix_two_ref[0]
    for load in loads[1:]:
        load.wait()
    for side in range(2):
        own, first, second = given[side * 3 : side * 3 + 3]
        new, new_first_ref, new_second_ref = made[1 + side], made[3 + side], made[5 + side]
        near = held[side]
        other = near[0].astype(jnp.float32)
        for level in range(1, levels):
            other = jnp.where(level_ref[0] == level, near[level].astype(jnp.float32), other)
        averaged = 0.5 * (own[...] + other)
        gradient = held[2 + side][...]
        new_first = beta_one * first[...] + (1.0 - beta_one) * gradient
        new_second = beta_two * second[...] + (1.0 - beta_two) * gradient * gradient
        stepped = new_first / fix_one / (jnp.sqrt(new_second / fix_two) + epsilon)
        new[...] = averaged - learn_rate * (stepped + weight_decay * averaged)
        new_first_ref[...] = new_first
        new_second_ref[...] = new_second
    loads[0].wait()


def adam(levels, level, fix_one, fix_two, *arrays):
    vmem = pl.BlockSpec(memory_space=pltpu.VMEM)
    smem = pl.BlockSpec(memory_space=pltpu.SMEM)
    hbm = pl.BlockSpec(memory_space=pl.ANY)
    comb, near_in, near_out, grad_in, grad_out = arrays[:5]
    f_in = jax.ShapeDtypeStruct(grad_in.shape, jnp.float32)
    f_out = jax.ShapeDtypeStruct(grad_out.shape, jnp.float32)
    return pl.pallas_call(
        partial(adam_kernel, levels),
        out_shape=(jax.ShapeDtypeStruct(comb.shape, comb.dtype), f_in, f_out, f_in, f_out, f_in, f_out),
        in_specs=[smem] * 3 + [hbm] * 5 + [vmem] * 6,
        out_specs=(vmem,) * 7,
        scratch_shapes=[
            pltpu.VMEM(one.shape, one.dtype) for one in (near_in, near_out, grad_in, grad_out)
        ]
        + [pltpu.SemaphoreType.DMA((5,))],
        compiler_params=pltpu.CompilerParams(vmem_limit_bytes=60 * 1024 * 1024),
    )(level, fix_one, fix_two, *arrays)


def per_device(
    tokens,
    cotangent,
    routes,
    router_pair_weight,
    capacity,
    training_step_index,
    frozen_gate_matrix,
    frozen_up_matrix,
    frozen_down_matrix,
    adapter_input_factor,
    adapter_output_factor,
    input_first_moment,
    output_first_moment,
    input_second_moment,
    output_second_moment,
):
    devices = lax.axis_size("exp")
    assert frozen_gate_matrix.shape[0] == 1 and devices == 16
    levels = lax.axis_size("rep").bit_length() - 1
    combined, grad_in, grad_out, near_in, near_out = layer(
        levels,
        capacity,
        routes[0].T,
        router_pair_weight[0].T,
        adapter_input_factor[0, 0],
        adapter_output_factor[0, 0],
        tokens[0],
        cotangent[0],
        frozen_gate_matrix[0],
        frozen_up_matrix[0],
        frozen_down_matrix[0],
    )
    level = training_step_index % levels
    power = (training_step_index + 1).astype(jnp.float32)
    fix_one = 1.0 - jnp.power(jnp.float32(beta_one), power)
    fix_two = 1.0 - jnp.power(jnp.float32(beta_two), power)
    results = adam(
        levels,
        level,
        fix_one,
        fix_two,
        combined,
        near_in,
        near_out,
        grad_in,
        grad_out,
        adapter_input_factor[0, 0],
        input_first_moment[0, 0],
        input_second_moment[0, 0],
        adapter_output_factor[0, 0],
        output_first_moment[0, 0],
        output_second_moment[0, 0],
    )
    return (results[0][None],) + tuple(one[None, None] for one in results[1:])


def solution(mesh):
    placed = (
        P("rep", "exp", None),
        P("rep", "exp", None),
        P("rep", "exp", None),
        P("rep", "exp", None),
        P(),
        P(),
        P("exp", None, None),
        P("exp", None, None),
        P("exp", None, None),
        P("rep", "exp", None, None),
        P("rep", "exp", None, None),
        P("rep", "exp", None, None),
        P("rep", "exp", None, None),
        P("rep", "exp", None, None),
        P("rep", "exp", None, None),
    )
    return jax.shard_map(
        per_device,
        mesh=mesh,
        in_specs=placed,
        out_specs=(
            P("rep", "exp", None),
            P("rep", "exp", None, None),
            P("rep", "exp", None, None),
            P("rep", "exp", None, None),
            P("rep", "exp", None, None),
            P("rep", "exp", None, None),
            P("rep", "exp", None, None),
        ),
        check_vma=False,
    )
```

```python
from functools import partial

import jax
import jax.numpy as jnp
from jax import lax
from jax.experimental import pallas as pl
from jax.experimental.pallas import tpu as pltpu
from jax.sharding import PartitionSpec as P

adapter_scale = 0.5
beta_one = 0.9
beta_two = 0.999
learn_rate = 0.02
weight_decay = 0.01
epsilon = 1e-08
MESH = pl.DeviceIdType.MESH
SIDE_OUT = 16
BACK_OUTER = 32
BACK_INNER = 48
PARTS_OUT = 2
PARTS_BACK = 2
OUTER = (
    "own", "kept", "fy10", "fs1", "fy11", "pair00", "fsx1", "fob0", "pair10", "fsx0", "fy20",
    "ty1", "post10", "cs10", "fy21", "fobx0", "fm20", "fs2", "pair11", "fm11", "pair20", "fy30",
    "post11", "fsx2", "cs11", "ty2", "post20", "post00", "cs20", "pair21", "fy31", "fs3", "fsx3",
    "ty0", "post21", "ym20", "cs21", "pair30", "ty3", "g12", "ym10", "fm30", "post30", "cs30",
    "pair31", "cm20", "ym21", "post31", "fm31", "fob3", "fm10", "cs31", "ym30", "fob1", "ym31",
    "ym11", "g13", "cm30", "pair01", "cm31", "post01", "fob2", "ym01", "ym00", "g10", "back", "g2",
    "cm21", "g11", "cm10", "ys", "fm21", "gout", "cm11", "gin", "fin2", "fin1",
)
INNER = (
    "own", "fsx1", "fm00", "fy20", "fm20", "kept", "fm21", "fy21", "fm01", "fs0", "pair10", "fs2",
    "pair00", "fy30", "ty1", "pair20", "fsx0", "fm30", "fy31", "fsx2", "ty2", "fm31", "pair11",
    "fs3", "fob1", "fy00", "post20", "pair21", "pair30", "fsx3", "fob0", "ty3", "fy01", "g12",
    "g11", "pair31", "post11", "fob3", "ym10", "fobx1", "cs20", "g10", "g13", "post00", "post31",
    "ty0", "post21", "post30", "ym21", "fob2", "ym20", "pair01", "ym30", "ym31", "back", "cs21",
    "cs30", "post01", "ym01", "cs31", "ym00", "cs00", "cs01", "cm30", "ys", "cm31", "cm20", "ym11",
    "cm00", "gin", "cm01", "cm21", "post10", "fin2", "g2", "gout", "fin1",
)


def cut_rows(rows, count, first=0):
    units = rows // 16
    ranges = []
    for one in range(count):
        size = 16 * (units // count + (1 if one < units % count else 0))
        ranges.append((first, first + size))
        first += size
    return ranges


def layer_kernel(
    levels,
    cap_ref,
    routes_ref,
    weight_ref,
    in_ref,
    out_ref,
    x_hbm,
    cot_hbm,
    gate_hbm,
    up_hbm,
    down_hbm,
    comb_ref,
    gin_ref,
    gout_ref,
    near_in_ref,
    near_out_ref,
    rows,
    part,
    from_core,
    from_y,
    from_ys,
    cm_in,
    cs_in,
    hid,
    gate_w,
    up_w,
    down_w,
    cots,
    in_b,
    outs,
    tables,
    kept,
    mine,
    mine_t,
    low_mine,
    low_got,
    back_mine,
    back_got,
    grad_mine,
    grad_got,
    grad_y,
    grad_yin,
    near_in,
    near_out,
    main_s,
    main_r,
    side_s,
    side_r,
    ob_s,
    ob_r,
    tile_s,
    tile_r,
    core_s,
    core_r,
    ym_s,
    ym_r,
    ys_s,
    ys_r,
    cm_s,
    cm_r,
    cs_s,
    cs_r,
    tab_s,
    tab_r,
    low_s,
    low_r,
    back_s,
    back_r,
    grad_s,
    grad_r,
    gy_s,
    gy_r,
    cot_s,
    cot_r,
    near_s,
    near_r,
    load_s,
):
    n = 16
    depth = 4
    pairs = n // 2
    f32 = jnp.float32
    bf16 = jnp.bfloat16
    me = lax.axis_index("exp")
    rep = lax.axis_index("rep")
    z, y, c = me // 4, (me // 2) % 2, me % 2
    home = me // 2
    tok = rows.shape[2]
    width = rows.shape[3]
    rank = in_ref.shape[0]
    cut_f = tok - SIDE_OUT
    out_parts = cut_rows(cut_f, PARTS_OUT)
    core_mate = me + 1 - 2 * c
    y_mate = me + 2 - 4 * y
    turned = z // 2
    sign = 1 - 2 * turned
    roles = ((z == 0) | (z == depth - 1), (z > 0) & (z < depth - 1))

    def real(zz):
        return 3 * turned + sign * zz

    def pair_of(zz, col):
        return real(zz) * 2 + (y if col == 0 else 1 - y)

    def cut_c(zz):
        return tok - (BACK_OUTER if zz in (0, depth - 1) else BACK_INNER)

    def back_parts(zz):
        return cut_rows(cut_c(zz), PARTS_BACK)

    def copy(src, dst, send, recv, device, axis="exp"):
        return pltpu.make_async_remote_copy(
            src_ref=src,
            dst_ref=dst,
            send_sem=send,
            recv_sem=recv,
            device_id={axis: device},
            device_id_type=MESH,
        )

    def towards(kind):
        return (me + 4 * sign, me - 4 * sign, y_mate)[kind]

    def moving(kind):
        return turned if kind == 0 else 1 - turned

    def main_to(kind, zz, part_at):
        lo, hi = out_parts[part_at]
        p = pair_of(zz, 0)
        block = rows.at[p, c, lo:hi]
        return copy(block, block, main_s.at[kind, zz, part_at], main_r.at[p, part_at], towards(kind))

    def main_in(zz, col, part_at):
        lo, hi = out_parts[part_at]
        p = pair_of(zz, col)
        block = rows.at[p, c, lo:hi]
        return copy(block, block, main_s.at[2, zz, part_at], main_r.at[p, part_at], y_mate)

    def side_to(kind, zz, col):
        p = pair_of(zz, col)
        block = rows.at[p, c, cut_f:tok]
        return copy(block, block, side_s.at[kind, zz * 2 + col], side_r.at[p], towards(kind))

    def ob_to(kind, zz, col):
        p = pair_of(zz, col)
        return copy(outs.at[p], outs.at[p], ob_s.at[kind, zz * 2 + col], ob_r.at[p], towards(kind))

    def tile_to(p):
        return copy(rows.at[p, c], rows.at[p, c], tile_s.at[p], tile_r.at[p], core_mate)

    def tile_in(p):
        return copy(rows.at[p, 1 - c], rows.at[p, 1 - c], tile_s.at[p], tile_r.at[p], core_mate)

    def core_to(p):
        return copy(part.at[p, 1 - c], from_core.at[p], core_s.at[p], core_r.at[p], core_mate)

    def ym_to(zz, part_at):
        lo, hi = back_parts(zz)[part_at]
        zt = real(zz)
        return copy(
            part.at[pair_of(zz, 1), c, lo:hi],
            from_y.at[zt, lo:hi],
            ym_s.at[zt, part_at],
            ym_r.at[zt, part_at],
            y_mate,
        )

    def ys_to(zz):
        size = tok - cut_c(zz)
        return copy(
            part.at[pair_of(zz, 1), c, cut_c(zz) : tok],
            from_ys.at[0:size],
            ys_s.at[0],
            ys_r.at[0],
            y_mate,
        )

    def cm_to(kind, zz, part_at):
        lo, hi = back_parts(zz)[part_at]
        zt = real(zz)
        return copy(
            part.at[pair_of(zz, 0), c, lo:hi],
            cm_in.at[moving(kind), zt, lo:hi],
            cm_s.at[zt, part_at],
            cm_r.at[moving(kind), zt, part_at],
            towards(kind),
        )

    def cs_to(kind, zz, col):
        p = pair_of(zz, col)
        size = tok - cut_c(zz)
        return copy(
            part.at[p, c, cut_c(zz) : tok],
            cs_in.at[moving(kind), p, 0:size],
            cs_s.at[p],
            cs_r.at[moving(kind), p],
            towards(kind),
        )

    def send_table(d):
        return copy(tables.at[me], tables.at[me], tab_s.at[d], tab_r.at[me], lax.rem(me + d, n))

    def send_low(p):
        return copy(low_mine.at[p], low_got.at[home], low_s.at[p], low_r.at[home], p * 2 + c)

    def send_back(p):
        return copy(back_mine.at[p], back_got.at[home], back_s.at[p], back_r.at[home], p * 2 + c)

    def send_grad(zz):
        zt = real(zz)
        return copy(grad_mine.at[zt], grad_got.at[z], grad_s.at[zt], grad_r.at[z], me + 4 * (zt - z))

    def send_grad_y():
        return copy(grad_y, grad_yin, gy_s.at[0], gy_r.at[0], y_mate)

    def send_cot():
        return copy(cots.at[c], cots.at[c], cot_s.at[0], cot_r.at[0], core_mate)

    def rep_mate(level):
        stride = 2**level
        return rep + stride * (1 - 2 * ((rep // stride) % 2))

    def send_near(level):
        return (
            copy(in_b, near_in.at[level], near_s.at[0, level], near_r.at[0, level], rep_mate(level), "rep"),
            copy(
                outs.at[home],
                near_out.at[level],
                near_s.at[1, level],
                near_r.at[1, level],
                rep_mate(level),
                "rep",
            ),
        )

    barrier = pltpu.get_barrier_semaphore()

    @pl.loop(1, n)
    def _(d):
        pl.semaphore_signal(
            barrier, inc=1, device_id={"exp": lax.rem(me + d, n)}, device_id_type=MESH
        )

    for level in range(levels):
        pl.semaphore_signal(
            barrier, inc=1, device_id={"rep": rep_mate(level)}, device_id_type=MESH
        )

    loads = [
        pltpu.make_async_copy(x_hbm, rows.at[home, c], load_s.at[0]),
        pltpu.make_async_copy(cot_hbm, cots.at[c], load_s.at[1]),
        pltpu.make_async_copy(gate_hbm, gate_w, load_s.at[2]),
        pltpu.make_async_copy(up_hbm, up_w, load_s.at[3]),
        pltpu.make_async_copy(down_hbm, down_w, load_s.at[4]),
    ]
    for load in loads:
        load.start()

    in_b[...] = in_ref[...].astype(bf16)
    outs[home] = out_ref[...].astype(bf16)
    expert = lax.broadcasted_iota(jnp.int32, (n, tok), 0)
    routed = routes_ref[...]
    weights = weight_ref[...].astype(f32)
    table = jnp.zeros((n, tok), f32)
    for k in range(routes_ref.shape[0]):
        table = table + jnp.where(routed[k : k + 1] == expert, weights[k : k + 1], 0.0)
    tables[me] = table.astype(bf16)

    pl.semaphore_wait(barrier, n - 1 + levels)
    loads[0].wait()

    def transposed_dot(a, b):
        return lax.dot_general(a, b, (((1,), (1,)), ((), ())), preferred_element_type=f32)

    def find_kept():
        for level in range(levels):
            for one in send_near(level):
                one.start()
        loads[1].wait()
        send_cot().start()

        @pl.loop(1, n)
        def _(d):
            source = lax.rem(me + d, n)
            copy(
                tables.at[source], tables.at[source], tab_s.at[d], tab_r.at[source], source
            ).wait_recv()

        later = lax.broadcasted_iota(jnp.int32, (tok, tok), 1)
        sooner = lax.broadcasted_iota(jnp.int32, (tok, tok), 0)
        strictly = (sooner < later).astype(bf16)
        which_expert = lax.broadcasted_iota(jnp.int32, (n, 1), 0)
        cap = jnp.zeros((n, 1), f32)
        for e in range(n):
            cap = jnp.where(which_expert == e, cap_ref[e].astype(f32), cap)
        all_weights = tables[...].astype(f32).reshape(n * n, tok)
        hits = (all_weights > 0).astype(f32)
        within = jnp.dot(hits.astype(bf16), strictly, preferred_element_type=f32)
        counts = jnp.sum(hits, axis=1, keepdims=True)
        before = jnp.zeros((n, 1), f32)
        for source in range(n):
            part_of = slice(source * n, (source + 1) * n)
            keep = before + within[part_of] < cap
            row = jnp.where(keep, all_weights[part_of], 0.0)
            kept[source] = row
            mine[source : source + 1, :] = jnp.sum(
                jnp.where(expert == me, row, 0.0), axis=0, keepdims=True
            )
            before = before + counts[part_of]
        mine_t[...] = mine[...].T
        copy(cots.at[1 - c], cots.at[1 - c], cot_s.at[0], cot_r.at[0], core_mate).wait_recv()
        for load in loads[2:]:
            load.wait()

    lane = lax.broadcasted_iota(jnp.int32, (tok, n), 1)

    def expert_pair(p):
        x = rows[p].reshape(2 * tok, width)
        gate = jnp.dot(x, gate_w[...], preferred_element_type=f32)
        upper = jnp.dot(x, up_w[...], preferred_element_type=f32)
        hidden = (gate / (1.0 + jnp.exp(-gate)) * upper).astype(bf16)
        hid[p] = hidden
        low_t = transposed_dot(in_b[...], hidden).astype(bf16).astype(f32)
        low = transposed_dot(hidden, in_b[...]).astype(bf16)
        result = jnp.dot(hidden, down_w[...], preferred_element_type=f32)
        result = result + adapter_scale * jnp.dot(low, outs[home], preferred_element_type=f32)
        for k in range(2):
            scale = jnp.sum(jnp.where(lane == p * 2 + k, mine_t[...], 0.0), axis=1, keepdims=True)
            part[p, k] = (scale * result[k * tok : (k + 1) * tok]).astype(bf16)
        core_to(p).start()
        weighted = jnp.concatenate(
            [low_t[:, k * tok : (k + 1) * tok] * mine[pl.ds(p * 2 + k, 1), :] for k in range(2)],
            axis=1,
        ).astype(bf16)

        @pl.when(p == home)
        def _():
            low_got[p] = weighted

        @pl.when(p != home)
        def _():
            low_mine[p] = weighted
            send_low(p).start()

    started = ([], [])

    def send(role, make):
        make().start()
        started[role].append(make)

    def spread(role, zz, make):
        for kind, goes in ((0, zz <= role), (1, zz >= role and role > 0)):
            if goes:
                send(role, partial(make, kind))

    def sources(role):
        return ((1,), (0, 1))[role]

    def add_up(target, base, p, lo, hi, others):
        @pl.loop(0, (hi - lo) // 16)
        def _(k):
            at = pl.multiple_of(k * 16, 16)
            total = part[p, c, pl.ds(lo + at, 16)].astype(f32)
            for one in others:
                total = total + one[pl.ds(at, 16)].astype(f32)
            target[pl.ds(base + at, 16)] = total.astype(bf16)

    def add_part(p, lo, hi, others):
        add_up(part.at[p, c], lo, p, lo, hi, others)

    def arrived(role, zz, h):
        if (zz, h) not in waited[role]:
            waited[role].append((zz, h))
            main_in(zz, 0, h).wait_recv()

    def step(role, name):
        word = name.rstrip("0123456789")
        digits = [int(one) for one in name[len(word) :]]
        zz = digits[0] if digits else role
        last = digits[1] if len(digits) > 1 else 0
        along = 0 if zz > role else 1
        if word == "own":

            @pl.loop(1, n)
            def _(d):
                send_table(d).start()

            send(role, lambda: side_to(2, role, 0))
            for h in range(PARTS_OUT):
                spread(role, role, lambda kind, h=h: main_to(kind, role, h))
                send(role, lambda h=h: main_to(2, role, h))
            spread(role, role, lambda kind: side_to(kind, role, 0))
            tile_to(home).start()
        elif word == "fob":
            if zz == role:
                send(role, lambda: ob_to(2, role, 0))
                spread(role, role, lambda kind: ob_to(kind, role, 0))
            else:
                for col in range(2):
                    ob_to(2, zz, col).wait_recv()
                for col in range(2):
                    spread(role, zz, lambda kind, col=col: ob_to(kind, zz, col))
        elif word == "fobx":
            ob_to(2, role, 1).wait_recv()
            spread(role, role, lambda kind: ob_to(kind, role, 1))
        elif word in ("fm", "fy"):
            arrived(role, zz, last)
            if word == "fm":
                spread(role, zz, lambda kind: main_to(kind, zz, last))
            else:
                send(role, lambda: main_to(2, zz, last))
        elif word == "fs":
            for h in range(PARTS_OUT):
                arrived(role, zz, h)
            side_to(2, zz, 0).wait_recv()
            spread(role, zz, lambda kind: side_to(kind, zz, 0))
            tile_to(pair_of(zz, 0)).start()
        elif word == "fsx":
            side_to(2, zz, 1).wait_recv()
            spread(role, zz, lambda kind: side_to(kind, zz, 1))
        elif word == "ty":
            for h in range(PARTS_OUT):
                main_in(zz, 1, h).wait_recv()
            tile_to(pair_of(zz, 1)).start()
        elif word == "post":
            p = pair_of(zz, last)
            core_to(p).wait_recv()
            add_part(p, 0, tok, [from_core.at[p]])
        elif word == "ym":
            send(role, lambda: ym_to(zz, last))
        elif word == "cs":
            if role == 1:
                p = pair_of(zz, last)
                cs_to(along, zz, last).wait_recv()
                lo = cut_c(zz)
                add_part(p, lo, tok, [cs_in.at[moving(along), p]])
            send(role, lambda: cs_to(along, zz, last))
        elif word == "cm":
            p, zt = pair_of(zz, 0), real(zz)
            lo, hi = back_parts(zz)[last]
            ym_to(zz, last).wait_recv()
            others = [from_y.at[zt, lo:hi]]
            if role == 1:
                cm_to(along, zz, last).wait_recv()
                others.append(cm_in.at[moving(along), zt, lo:hi])
            add_part(p, lo, hi, others)
            send(role, lambda: cm_to(along, zz, last))
        elif word == "ys":
            p = pair_of(role, 1)
            lo = cut_c(role)
            for kind in sources(role):
                cs_to(kind, role, 1).wait_recv()
            add_part(p, lo, tok, [cs_in.at[moving(kind), p] for kind in sources(role)])
            send(role, lambda: ys_to(role))
        elif word == "fin":
            if name == "fin1":
                lo, hi = 0, cut_c(role)
                for h in range(PARTS_BACK):
                    ym_to(role, h).wait_recv()
                    for kind in sources(role):
                        cm_to(kind, role, h).wait_recv()
                others = [from_y.at[z, lo:hi]]
                others += [cm_in.at[moving(k), z, lo:hi] for k in sources(role)]
            else:
                lo, hi = cut_c(role), tok
                ys_to(role).wait_recv()
                for kind in sources(role):
                    cs_to(kind, role, 0).wait_recv()
                others = [from_ys] + [cs_in.at[moving(k), home] for k in sources(role)]
            add_up(comb_ref, lo, home, lo, hi, others)
        elif word == "g":
            if name == "g2":
                for k in range(depth):
                    if k != role:
                        source = real(k)
                        copy(
                            grad_mine.at[source],
                            grad_got.at[source],
                            grad_s.at[source],
                            grad_r.at[source],
                            y_mate,
                        ).wait_recv()
                total = grad_got[0, 1 - y].astype(f32)
                for k in range(1, depth):
                    total = total + grad_got[k, 1 - y].astype(f32)
                grad_y[...] = total.astype(bf16)
                send(role, send_grad_y)
            else:
                zt = real(last)
                for col in range(2):
                    if last != role or col == 1:
                        p = pair_of(last, col)
                        copy(
                            low_mine.at[p], low_got.at[p], low_s.at[p], low_r.at[p], p * 2 + c
                        ).wait_recv()
                both = low_got[pl.ds(zt * 2, 2)].reshape(2 * rank, 2 * tok)
                grads = adapter_scale * jnp.dot(
                    both, cots[...].reshape(2 * tok, width), preferred_element_type=f32
                )
                grads = grads.astype(bf16).reshape(2, rank, width)
                if last == role:
                    grad_got[zt] = grads
                else:
                    grad_mine[zt] = grads
                    send(role, lambda: send_grad(last))
        elif word == "back":
            both = cots[...].reshape(2 * tok, width)
            returned = transposed_dot(outs[...].reshape(pairs * rank, width), both)
            for p in range(pairs):
                weight = jnp.concatenate(
                    [kept[home * 2 + k, pl.ds(p * 2 + c, 1), :] for k in range(2)], axis=1
                )
                back_mine[p] = (returned[p * rank : (p + 1) * rank] * weight).astype(bf16)

            back_got[home] = back_mine[home]

            @pl.loop(0, pairs)
            def _(p):
                @pl.when(p != home)
                def _():
                    send_back(p).start()

        elif word == "gin":
            gin_ref[...] = jnp.zeros_like(gin_ref)

            @pl.loop(0, pairs)
            def _(p):
                @pl.when(p != home)
                def _():
                    copy(
                        back_mine.at[p], back_got.at[p], back_s.at[p], back_r.at[p], p * 2 + c
                    ).wait_recv()

                gin_ref[...] += adapter_scale * jnp.dot(
                    back_got[p], hid[p], preferred_element_type=f32
                )

        elif word == "gout":
            send_grad_y().wait_recv()
            total = grad_yin[...].astype(f32)
            for k in range(depth):
                total = total + grad_got[k, y].astype(f32)
            gout_ref[...] = total
        else:
            raise ValueError(name)

    waited = ([], [])
    plans = (OUTER, INNER)
    begin = [plan.index("kept") for plan in plans]
    computes = [[one for one in plan if one.startswith("pair")] for plan in plans]

    def steps(role, names):
        for name in names:
            step(role, name)

    def between(role, k):
        plan = plans[role]
        lo = begin[role] if k == 0 else plan.index(computes[role][k - 1])
        hi = plan.index(computes[role][k]) if k < pairs else len(plan)
        return plan[lo + 1 : hi]

    for role in range(2):
        pl.when(roles[role])(partial(steps, role, plans[role][: begin[role]]))
    find_kept()

    @pl.loop(0, pairs)
    def _(i):
        for k in range(pairs):
            for role in range(2):
                pl.when(roles[role] & (i == k))(partial(steps, role, between(role, k)))
        p = i * 0
        for role in range(2):
            for k in range(pairs):
                zz, col = (int(one) for one in computes[role][k][-2:])
                p = jnp.where(roles[role] & (i == k), pair_of(zz, col), p)
        tile_in(p).wait_recv()
        expert_pair(p)

    for role in range(2):
        pl.when(roles[role])(partial(steps, role, between(role, pairs)))

    for level in range(levels):
        for one in send_near(level):
            one.wait_recv()
    near_in_ref[...] = near_in[...]
    near_out_ref[...] = near_out[...]

    def sent(role):
        for make in started[role]:
            make().wait_send()

    for role in range(2):
        pl.when(roles[role])(partial(sent, role))
    send_cot().wait_send()

    @pl.loop(0, pairs)
    def _(p):
        tile_to(p).wait_send()
        core_to(p).wait_send()

        @pl.when(p != home)
        def _():
            send_low(p).wait_send()
            send_back(p).wait_send()

    @pl.loop(1, n)
    def _(d):
        send_table(d).wait_send()

    for level in range(levels):
        for one in send_near(level):
            one.wait_send()


def layer(levels, cap, routes, weights, in_f, out_f, x, cot, gate, up, down):
    n = cap.shape[0]
    tok, width = cot.shape
    rank, units = in_f.shape
    pairs, depth = n // 2, n // 4
    vmem = pl.BlockSpec(memory_space=pltpu.VMEM)
    hbm = pl.BlockSpec(memory_space=pl.ANY)
    bf16 = jnp.bfloat16
    f32 = jnp.float32
    dma = pltpu.SemaphoreType.DMA
    main, side = tok - min(BACK_OUTER, BACK_INNER), max(BACK_OUTER, BACK_INNER)
    return pl.pallas_call(
        partial(layer_kernel, levels),
        out_shape=(
            pltpu.VMEM((tok, width), bf16),
            pltpu.VMEM((rank, units), f32),
            pltpu.VMEM((rank, width), f32),
            pltpu.VMEM((levels, rank, units), bf16),
            pltpu.VMEM((levels, rank, width), bf16),
        ),
        in_specs=[pl.BlockSpec(memory_space=pltpu.SMEM)] + [vmem] * 4 + [hbm] * 5,
        out_specs=(vmem,) * 5,
        scratch_shapes=[
            pltpu.VMEM((pairs, 2, tok, width), bf16),
            pltpu.VMEM((pairs, 2, tok, width), bf16),
            pltpu.VMEM((pairs, tok, width), bf16),
            pltpu.VMEM((depth, main, width), bf16),
            pltpu.VMEM((side, width), bf16),
            pltpu.VMEM((2, depth, main, width), bf16),
            pltpu.VMEM((2, pairs, side, width), bf16),
            pltpu.VMEM((pairs, 2 * tok, units), bf16),
            pltpu.VMEM((width, units), bf16),
            pltpu.VMEM((width, units), bf16),
            pltpu.VMEM((units, width), bf16),
            pltpu.VMEM((2, tok, width), bf16),
            pltpu.VMEM((rank, units), bf16),
            pltpu.VMEM((pairs, rank, width), bf16),
            pltpu.VMEM((n, n, tok), bf16),
            pltpu.VMEM((n, n, tok), f32),
            pltpu.VMEM((n, tok), f32),
            pltpu.VMEM((tok, n), f32),
            pltpu.VMEM((pairs, rank, 2 * tok), bf16),
            pltpu.VMEM((pairs, rank, 2 * tok), bf16),
            pltpu.VMEM((pairs, rank, 2 * tok), bf16),
            pltpu.VMEM((pairs, rank, 2 * tok), bf16),
            pltpu.VMEM((depth, 2, rank, width), bf16),
            pltpu.VMEM((depth, 2, rank, width), bf16),
            pltpu.VMEM((rank, width), bf16),
            pltpu.VMEM((rank, width), bf16),
            pltpu.VMEM((levels, rank, units), bf16),
            pltpu.VMEM((levels, rank, width), bf16),
            dma((3, depth, PARTS_OUT)),
            dma((pairs, PARTS_OUT)),
            dma((3, pairs)),
            dma((pairs,)),
            dma((3, pairs)),
            dma((pairs,)),
            dma((pairs,)),
            dma((pairs,)),
            dma((pairs,)),
            dma((pairs,)),
            dma((depth, PARTS_BACK)),
            dma((depth, PARTS_BACK)),
            dma((1,)),
            dma((1,)),
            dma((depth, PARTS_BACK)),
            dma((2, depth, PARTS_BACK)),
            dma((pairs,)),
            dma((2, pairs)),
            dma((n,)),
            dma((n,)),
            dma((pairs,)),
            dma((pairs,)),
            dma((pairs,)),
            dma((pairs,)),
            dma((depth,)),
            dma((depth,)),
            dma((1,)),
            dma((1,)),
            dma((1,)),
            dma((1,)),
            dma((2, levels)),
            dma((2, levels)),
            dma((5,)),
        ],
        compiler_params=pltpu.CompilerParams(
            collective_id=0, has_side_effects=True, vmem_limit_bytes=56 * 1024 * 1024
        ),
        cost_estimate=pl.CostEstimate(
            flops=20_000_000_000, bytes_accessed=30_000_000, transcendentals=0
        ),
    )(cap, routes, weights, in_f, out_f, x, cot, gate, up, down)


def adam_kernel(levels, level_ref, fix_one_ref, fix_two_ref, *refs):
    comb, near_in, near_out, grad_in, grad_out = refs[:5]
    given, made, done = refs[5:11], refs[11:18], refs[18]
    out = pltpu.make_async_copy(comb, made[0], done)
    out.start()
    fix_one, fix_two = fix_one_ref[0], fix_two_ref[0]
    for side in range(2):
        own, first, second = given[side * 3 : side * 3 + 3]
        new, new_first_ref, new_second_ref = made[1 + side], made[3 + side], made[5 + side]
        near = (near_in, near_out)[side]
        other = near[0].astype(jnp.float32)
        for level in range(1, levels):
            other = jnp.where(level_ref[0] == level, near[level].astype(jnp.float32), other)
        averaged = 0.5 * (own[...] + other)
        gradient = (grad_in, grad_out)[side][...]
        new_first = beta_one * first[...] + (1.0 - beta_one) * gradient
        new_second = beta_two * second[...] + (1.0 - beta_two) * gradient * gradient
        stepped = new_first / fix_one / (jnp.sqrt(new_second / fix_two) + epsilon)
        new[...] = averaged - learn_rate * (stepped + weight_decay * averaged)
        new_first_ref[...] = new_first
        new_second_ref[...] = new_second
    out.wait()


def adam(levels, level, fix_one, fix_two, *arrays):
    vmem = pl.BlockSpec(memory_space=pltpu.VMEM)
    smem = pl.BlockSpec(memory_space=pltpu.SMEM)
    hbm = pl.BlockSpec(memory_space=pl.ANY)
    comb, near_in, near_out, grad_in, grad_out = arrays[:5]
    f_in = jax.ShapeDtypeStruct(grad_in.shape, jnp.float32)
    f_out = jax.ShapeDtypeStruct(grad_out.shape, jnp.float32)
    return pl.pallas_call(
        partial(adam_kernel, levels),
        out_shape=(jax.ShapeDtypeStruct(comb.shape, comb.dtype), f_in, f_out, f_in, f_out, f_in, f_out),
        in_specs=[smem] * 3 + [vmem] * 11,
        out_specs=(hbm,) + (vmem,) * 6,
        scratch_shapes=[pltpu.SemaphoreType.DMA],
        compiler_params=pltpu.CompilerParams(vmem_limit_bytes=8 * 1024 * 1024),
    )(level, fix_one, fix_two, *arrays)


def per_device(
    tokens,
    cotangent,
    routes,
    router_pair_weight,
    capacity,
    training_step_index,
    frozen_gate_matrix,
    frozen_up_matrix,
    frozen_down_matrix,
    adapter_input_factor,
    adapter_output_factor,
    input_first_moment,
    output_first_moment,
    input_second_moment,
    output_second_moment,
):
    devices = lax.axis_size("exp")
    assert frozen_gate_matrix.shape[0] == 1 and devices == 16
    levels = lax.axis_size("rep").bit_length() - 1
    combined, grad_in, grad_out, near_in, near_out = layer(
        levels,
        capacity,
        routes[0].T,
        router_pair_weight[0].T,
        adapter_input_factor[0, 0],
        adapter_output_factor[0, 0],
        tokens[0],
        cotangent[0],
        frozen_gate_matrix[0],
        frozen_up_matrix[0],
        frozen_down_matrix[0],
    )
    level = training_step_index % levels
    power = (training_step_index + 1).astype(jnp.float32)
    fix_one = 1.0 - jnp.power(jnp.float32(beta_one), power)
    fix_two = 1.0 - jnp.power(jnp.float32(beta_two), power)
    results = adam(
        levels,
        level,
        fix_one,
        fix_two,
        combined,
        near_in,
        near_out,
        grad_in,
        grad_out,
        adapter_input_factor[0, 0],
        input_first_moment[0, 0],
        input_second_moment[0, 0],
        adapter_output_factor[0, 0],
        output_first_moment[0, 0],
        output_second_moment[0, 0],
    )
    return (results[0][None],) + tuple(one[None, None] for one in results[1:])


def solution(mesh):
    placed = (
        P("rep", "exp", None),
        P("rep", "exp", None),
        P("rep", "exp", None),
        P("rep", "exp", None),
        P(),
        P(),
        P("exp", None, None),
        P("exp", None, None),
        P("exp", None, None),
        P("rep", "exp", None, None),
        P("rep", "exp", None, None),
        P("rep", "exp", None, None),
        P("rep", "exp", None, None),
        P("rep", "exp", None, None),
        P("rep", "exp", None, None),
    )
    return jax.shard_map(
        per_device,
        mesh=mesh,
        in_specs=placed,
        out_specs=(
            P("rep", "exp", None),
            P("rep", "exp", None, None),
            P("rep", "exp", None, None),
            P("rep", "exp", None, None),
            P("rep", "exp", None, None),
            P("rep", "exp", None, None),
            P("rep", "exp", None, None),
        ),
        check_vma=False,
    )
```

```python
from functools import partial

import jax
import jax.numpy as jnp
from jax import lax
from jax.experimental import pallas as pl
from jax.experimental.pallas import tpu as pltpu
from jax.sharding import PartitionSpec as P

adapter_scale = 0.5
beta_one = 0.9
beta_two = 0.999
learn_rate = 0.02
weight_decay = 0.01
epsilon = 1e-08
MESH = pl.DeviceIdType.MESH
SIDE_OUT = 16
BACK_OUTER = 32
BACK_INNER = 48
PARTS_OUT = 2
PARTS_BACK = 2
OUTER = (
    "own", "kept", "fy10", "fs1", "fy11", "pair00", "fsx1", "fob0", "pair10", "fsx0", "fy20",
    "ty1", "post10", "cs10", "fy21", "fobx0", "fm20", "fs2", "pair11", "fm11", "pair20", "fy30",
    "post11", "fsx2", "cs11", "ty2", "post20", "post00", "cs20", "pair21", "fy31", "fs3", "fsx3",
    "ty0", "post21", "ym20", "cs21", "pair30", "ty3", "g12", "ym10", "fm30", "post30", "cs30",
    "pair31", "cm20", "ym21", "post31", "fm31", "fob3", "fm10", "cs31", "ym30", "fob1", "ym31",
    "ym11", "g13", "cm30", "pair01", "cm31", "post01", "fob2", "ym01", "ym00", "g10", "back", "g2",
    "cm21", "g11", "cm10", "ys", "fm21", "gout", "cm11", "gin", "fin2", "fin1",
)
INNER = (
    "own", "fsx1", "fm00", "fy20", "fm20", "kept", "fm21", "fy21", "fm01", "fs0", "pair10", "fs2",
    "pair00", "fy30", "ty1", "pair20", "fsx0", "fm30", "fy31", "fsx2", "ty2", "fm31", "pair11",
    "fs3", "fob1", "fy00", "post20", "pair21", "pair30", "fsx3", "fob0", "ty3", "fy01", "g12",
    "g11", "pair31", "post11", "fob3", "ym10", "fobx1", "cs20", "g10", "g13", "post00", "post31",
    "ty0", "post21", "post30", "ym21", "fob2", "ym20", "pair01", "ym30", "ym31", "back", "cs21",
    "cs30", "post01", "ym01", "cs31", "ym00", "cs00", "cs01", "cm30", "ys", "cm31", "cm20", "ym11",
    "cm00", "gin", "cm01", "cm21", "post10", "fin2", "g2", "gout", "fin1",
)


def cut_rows(rows, count, first=0):
    units = rows // 16
    ranges = []
    for one in range(count):
        size = 16 * (units // count + (1 if one < units % count else 0))
        ranges.append((first, first + size))
        first += size
    return ranges


def layer_kernel(
    levels,
    cap_ref,
    routes_hbm,
    weight_hbm,
    in_hbm,
    out_hbm,
    x_hbm,
    cot_hbm,
    gate_hbm,
    up_hbm,
    down_hbm,
    comb_ref,
    gin_ref,
    gout_ref,
    near_in_ref,
    near_out_ref,
    rows,
    part,
    from_core,
    from_y,
    from_ys,
    cm_in,
    cs_in,
    hid,
    gate_w,
    up_w,
    down_w,
    cots,
    in_b,
    outs,
    tables,
    kept,
    mine,
    mine_t,
    low_mine,
    low_got,
    back_mine,
    back_got,
    grad_mine,
    grad_got,
    grad_y,
    grad_yin,
    near_in,
    near_out,
    routes_ref,
    weight_ref,
    in_ref,
    out_ref,
    main_s,
    main_r,
    side_s,
    side_r,
    ob_s,
    ob_r,
    tile_s,
    tile_r,
    core_s,
    core_r,
    ym_s,
    ym_r,
    ys_s,
    ys_r,
    cm_s,
    cm_r,
    cs_s,
    cs_r,
    tab_s,
    tab_r,
    low_s,
    low_r,
    back_s,
    back_r,
    grad_s,
    grad_r,
    gy_s,
    gy_r,
    cot_s,
    cot_r,
    near_s,
    near_r,
    load_s,
):
    n = 16
    depth = 4
    pairs = n // 2
    f32 = jnp.float32
    bf16 = jnp.bfloat16
    me = lax.axis_index("exp")
    rep = lax.axis_index("rep")
    z, y, c = me // 4, (me // 2) % 2, me % 2
    home = me // 2
    tok = rows.shape[2]
    width = rows.shape[3]
    rank = outs.shape[1]
    cut_f = tok - SIDE_OUT
    out_parts = cut_rows(cut_f, PARTS_OUT)
    core_mate = me + 1 - 2 * c
    y_mate = me + 2 - 4 * y
    turned = z // 2
    sign = 1 - 2 * turned
    roles = ((z == 0) | (z == depth - 1), (z > 0) & (z < depth - 1))

    def real(zz):
        return 3 * turned + sign * zz

    def pair_of(zz, col):
        return real(zz) * 2 + (y if col == 0 else 1 - y)

    def cut_c(zz):
        return tok - (BACK_OUTER if zz in (0, depth - 1) else BACK_INNER)

    def back_parts(zz):
        return cut_rows(cut_c(zz), PARTS_BACK)

    def copy(src, dst, send, recv, device, axis="exp"):
        return pltpu.make_async_remote_copy(
            src_ref=src,
            dst_ref=dst,
            send_sem=send,
            recv_sem=recv,
            device_id={axis: device},
            device_id_type=MESH,
        )

    def towards(kind):
        return (me + 4 * sign, me - 4 * sign, y_mate)[kind]

    def moving(kind):
        return turned if kind == 0 else 1 - turned

    def main_to(kind, zz, part_at):
        lo, hi = out_parts[part_at]
        p = pair_of(zz, 0)
        block = rows.at[p, c, lo:hi]
        return copy(block, block, main_s.at[kind, zz, part_at], main_r.at[p, part_at], towards(kind))

    def main_in(zz, col, part_at):
        lo, hi = out_parts[part_at]
        p = pair_of(zz, col)
        block = rows.at[p, c, lo:hi]
        return copy(block, block, main_s.at[2, zz, part_at], main_r.at[p, part_at], y_mate)

    def side_to(kind, zz, col):
        p = pair_of(zz, col)
        block = rows.at[p, c, cut_f:tok]
        return copy(block, block, side_s.at[kind, zz * 2 + col], side_r.at[p], towards(kind))

    def ob_to(kind, zz, col):
        p = pair_of(zz, col)
        return copy(outs.at[p], outs.at[p], ob_s.at[kind, zz * 2 + col], ob_r.at[p], towards(kind))

    def tile_to(p):
        return copy(rows.at[p, c], rows.at[p, c], tile_s.at[p], tile_r.at[p], core_mate)

    def tile_in(p):
        return copy(rows.at[p, 1 - c], rows.at[p, 1 - c], tile_s.at[p], tile_r.at[p], core_mate)

    def core_to(p):
        return copy(part.at[p, 1 - c], from_core.at[p], core_s.at[p], core_r.at[p], core_mate)

    def ym_to(zz, part_at):
        lo, hi = back_parts(zz)[part_at]
        zt = real(zz)
        return copy(
            part.at[pair_of(zz, 1), c, lo:hi],
            from_y.at[zt, lo:hi],
            ym_s.at[zt, part_at],
            ym_r.at[zt, part_at],
            y_mate,
        )

    def ys_to(zz):
        size = tok - cut_c(zz)
        return copy(
            part.at[pair_of(zz, 1), c, cut_c(zz) : tok],
            from_ys.at[0:size],
            ys_s.at[0],
            ys_r.at[0],
            y_mate,
        )

    def cm_to(kind, zz, part_at):
        lo, hi = back_parts(zz)[part_at]
        zt = real(zz)
        return copy(
            part.at[pair_of(zz, 0), c, lo:hi],
            cm_in.at[moving(kind), zt, lo:hi],
            cm_s.at[zt, part_at],
            cm_r.at[moving(kind), zt, part_at],
            towards(kind),
        )

    def cs_to(kind, zz, col):
        p = pair_of(zz, col)
        size = tok - cut_c(zz)
        return copy(
            part.at[p, c, cut_c(zz) : tok],
            cs_in.at[moving(kind), p, 0:size],
            cs_s.at[p],
            cs_r.at[moving(kind), p],
            towards(kind),
        )

    def send_table(d):
        return copy(tables.at[me], tables.at[me], tab_s.at[d], tab_r.at[me], lax.rem(me + d, n))

    def send_low(p):
        return copy(low_mine.at[p], low_got.at[home], low_s.at[p], low_r.at[home], p * 2 + c)

    def send_back(p):
        return copy(back_mine.at[p], back_got.at[home], back_s.at[p], back_r.at[home], p * 2 + c)

    def send_grad(zz):
        zt = real(zz)
        return copy(grad_mine.at[zt], grad_got.at[z], grad_s.at[zt], grad_r.at[z], me + 4 * (zt - z))

    def send_grad_y():
        return copy(grad_y, grad_yin, gy_s.at[0], gy_r.at[0], y_mate)

    def send_cot():
        return copy(cots.at[c], cots.at[c], cot_s.at[0], cot_r.at[0], core_mate)

    def rep_mate(level):
        stride = 2**level
        return rep + stride * (1 - 2 * ((rep // stride) % 2))

    def send_near(level):
        return (
            copy(in_b, near_in.at[level], near_s.at[0, level], near_r.at[0, level], rep_mate(level), "rep"),
            copy(
                outs.at[home],
                near_out.at[level],
                near_s.at[1, level],
                near_r.at[1, level],
                rep_mate(level),
                "rep",
            ),
        )

    barrier = pltpu.get_barrier_semaphore()

    @pl.loop(1, n)
    def _(d):
        pl.semaphore_signal(
            barrier, inc=1, device_id={"exp": lax.rem(me + d, n)}, device_id_type=MESH
        )

    for level in range(levels):
        pl.semaphore_signal(
            barrier, inc=1, device_id={"rep": rep_mate(level)}, device_id_type=MESH
        )

    loads = [
        pltpu.make_async_copy(x_hbm, rows.at[home, c], load_s.at[0]),
        pltpu.make_async_copy(cot_hbm, cots.at[c], load_s.at[1]),
        pltpu.make_async_copy(gate_hbm, gate_w, load_s.at[2]),
        pltpu.make_async_copy(up_hbm, up_w, load_s.at[3]),
        pltpu.make_async_copy(down_hbm, down_w, load_s.at[4]),
    ]
    small = [
        pltpu.make_async_copy(source, target, load_s.at[5 + k])
        for k, (source, target) in enumerate(
            (
                (routes_hbm, routes_ref),
                (weight_hbm, weight_ref),
                (in_hbm, in_ref),
                (out_hbm, out_ref),
            )
        )
    ]
    for load in small + loads:
        load.start()
    for load in small:
        load.wait()

    in_b[...] = in_ref[...].astype(bf16)
    outs[home] = out_ref[...].astype(bf16)
    expert = lax.broadcasted_iota(jnp.int32, (n, tok), 0)
    routed = routes_ref[...]
    weights = weight_ref[...].astype(f32)
    table = jnp.zeros((n, tok), f32)
    for k in range(routes_ref.shape[0]):
        table = table + jnp.where(routed[k : k + 1] == expert, weights[k : k + 1], 0.0)
    tables[me] = table.astype(bf16)

    pl.semaphore_wait(barrier, n - 1 + levels)
    loads[0].wait()

    def transposed_dot(a, b):
        return lax.dot_general(a, b, (((1,), (1,)), ((), ())), preferred_element_type=f32)

    def find_kept():
        for level in range(levels):
            for one in send_near(level):
                one.start()
        loads[1].wait()
        send_cot().start()

        @pl.loop(1, n)
        def _(d):
            source = lax.rem(me + d, n)
            copy(
                tables.at[source], tables.at[source], tab_s.at[d], tab_r.at[source], source
            ).wait_recv()

        later = lax.broadcasted_iota(jnp.int32, (tok, tok), 1)
        sooner = lax.broadcasted_iota(jnp.int32, (tok, tok), 0)
        strictly = (sooner < later).astype(bf16)
        which_expert = lax.broadcasted_iota(jnp.int32, (n, 1), 0)
        cap = jnp.zeros((n, 1), f32)
        for e in range(n):
            cap = jnp.where(which_expert == e, cap_ref[e].astype(f32), cap)
        all_weights = tables[...].astype(f32).reshape(n * n, tok)
        hits = (all_weights > 0).astype(f32)
        within = jnp.dot(hits.astype(bf16), strictly, preferred_element_type=f32)
        counts = jnp.sum(hits, axis=1, keepdims=True)
        before = jnp.zeros((n, 1), f32)
        for source in range(n):
            part_of = slice(source * n, (source + 1) * n)
            keep = before + within[part_of] < cap
            row = jnp.where(keep, all_weights[part_of], 0.0)
            kept[source] = row
            mine[source : source + 1, :] = jnp.sum(
                jnp.where(expert == me, row, 0.0), axis=0, keepdims=True
            )
            before = before + counts[part_of]
        mine_t[...] = mine[...].T
        copy(cots.at[1 - c], cots.at[1 - c], cot_s.at[0], cot_r.at[0], core_mate).wait_recv()
        for load in loads[2:]:
            load.wait()

    lane = lax.broadcasted_iota(jnp.int32, (tok, n), 1)

    def expert_pair(p):
        x = rows[p].reshape(2 * tok, width)
        gate = jnp.dot(x, gate_w[...], preferred_element_type=f32)
        upper = jnp.dot(x, up_w[...], preferred_element_type=f32)
        hidden = (gate / (1.0 + jnp.exp(-gate)) * upper).astype(bf16)
        hid[p] = hidden
        low_t = transposed_dot(in_b[...], hidden).astype(bf16).astype(f32)
        low = transposed_dot(hidden, in_b[...]).astype(bf16)
        result = jnp.dot(hidden, down_w[...], preferred_element_type=f32)
        result = result + adapter_scale * jnp.dot(low, outs[home], preferred_element_type=f32)
        for k in range(2):
            scale = jnp.sum(jnp.where(lane == p * 2 + k, mine_t[...], 0.0), axis=1, keepdims=True)
            part[p, k] = (scale * result[k * tok : (k + 1) * tok]).astype(bf16)
        core_to(p).start()
        weighted = jnp.concatenate(
            [low_t[:, k * tok : (k + 1) * tok] * mine[pl.ds(p * 2 + k, 1), :] for k in range(2)],
            axis=1,
        ).astype(bf16)

        @pl.when(p == home)
        def _():
            low_got[p] = weighted

        @pl.when(p != home)
        def _():
            low_mine[p] = weighted
            send_low(p).start()

    started = ([], [])

    def send(role, make):
        make().start()
        started[role].append(make)

    def spread(role, zz, make):
        for kind, goes in ((0, zz <= role), (1, zz >= role and role > 0)):
            if goes:
                send(role, partial(make, kind))

    def sources(role):
        return ((1,), (0, 1))[role]

    def add_up(target, base, p, lo, hi, others):
        @pl.loop(0, (hi - lo) // 16)
        def _(k):
            at = pl.multiple_of(k * 16, 16)
            total = part[p, c, pl.ds(lo + at, 16)].astype(f32)
            for one in others:
                total = total + one[pl.ds(at, 16)].astype(f32)
            target[pl.ds(base + at, 16)] = total.astype(bf16)

    def add_part(p, lo, hi, others):
        add_up(part.at[p, c], lo, p, lo, hi, others)

    def arrived(role, zz, h):
        if (zz, h) not in waited[role]:
            waited[role].append((zz, h))
            main_in(zz, 0, h).wait_recv()

    def step(role, name):
        word = name.rstrip("0123456789")
        digits = [int(one) for one in name[len(word) :]]
        zz = digits[0] if digits else role
        last = digits[1] if len(digits) > 1 else 0
        along = 0 if zz > role else 1
        if word == "own":

            @pl.loop(1, n)
            def _(d):
                send_table(d).start()

            send(role, lambda: side_to(2, role, 0))
            for h in range(PARTS_OUT):
                spread(role, role, lambda kind, h=h: main_to(kind, role, h))
                send(role, lambda h=h: main_to(2, role, h))
            spread(role, role, lambda kind: side_to(kind, role, 0))
            tile_to(home).start()
        elif word == "fob":
            if zz == role:
                send(role, lambda: ob_to(2, role, 0))
                spread(role, role, lambda kind: ob_to(kind, role, 0))
            else:
                for col in range(2):
                    ob_to(2, zz, col).wait_recv()
                for col in range(2):
                    spread(role, zz, lambda kind, col=col: ob_to(kind, zz, col))
        elif word == "fobx":
            ob_to(2, role, 1).wait_recv()
            spread(role, role, lambda kind: ob_to(kind, role, 1))
        elif word in ("fm", "fy"):
            arrived(role, zz, last)
            if word == "fm":
                spread(role, zz, lambda kind: main_to(kind, zz, last))
            else:
                send(role, lambda: main_to(2, zz, last))
        elif word == "fs":
            for h in range(PARTS_OUT):
                arrived(role, zz, h)
            side_to(2, zz, 0).wait_recv()
            spread(role, zz, lambda kind: side_to(kind, zz, 0))
            tile_to(pair_of(zz, 0)).start()
        elif word == "fsx":
            side_to(2, zz, 1).wait_recv()
            spread(role, zz, lambda kind: side_to(kind, zz, 1))
        elif word == "ty":
            for h in range(PARTS_OUT):
                main_in(zz, 1, h).wait_recv()
            tile_to(pair_of(zz, 1)).start()
        elif word == "post":
            p = pair_of(zz, last)
            core_to(p).wait_recv()
            add_part(p, 0, tok, [from_core.at[p]])
        elif word == "ym":
            send(role, lambda: ym_to(zz, last))
        elif word == "cs":
            if role == 1:
                p = pair_of(zz, last)
                cs_to(along, zz, last).wait_recv()
                lo = cut_c(zz)
                add_part(p, lo, tok, [cs_in.at[moving(along), p]])
            send(role, lambda: cs_to(along, zz, last))
        elif word == "cm":
            p, zt = pair_of(zz, 0), real(zz)
            lo, hi = back_parts(zz)[last]
            ym_to(zz, last).wait_recv()
            others = [from_y.at[zt, lo:hi]]
            if role == 1:
                cm_to(along, zz, last).wait_recv()
                others.append(cm_in.at[moving(along), zt, lo:hi])
            add_part(p, lo, hi, others)
            send(role, lambda: cm_to(along, zz, last))
        elif word == "ys":
            p = pair_of(role, 1)
            lo = cut_c(role)
            for kind in sources(role):
                cs_to(kind, role, 1).wait_recv()
            add_part(p, lo, tok, [cs_in.at[moving(kind), p] for kind in sources(role)])
            send(role, lambda: ys_to(role))
        elif word == "fin":
            if name == "fin1":
                lo, hi = 0, cut_c(role)
                for h in range(PARTS_BACK):
                    ym_to(role, h).wait_recv()
                    for kind in sources(role):
                        cm_to(kind, role, h).wait_recv()
                others = [from_y.at[z, lo:hi]]
                others += [cm_in.at[moving(k), z, lo:hi] for k in sources(role)]
            else:
                lo, hi = cut_c(role), tok
                ys_to(role).wait_recv()
                for kind in sources(role):
                    cs_to(kind, role, 0).wait_recv()
                others = [from_ys] + [cs_in.at[moving(k), home] for k in sources(role)]
            add_up(comb_ref, lo, home, lo, hi, others)
        elif word == "g":
            if name == "g2":
                for k in range(depth):
                    if k != role:
                        source = real(k)
                        copy(
                            grad_mine.at[source],
                            grad_got.at[source],
                            grad_s.at[source],
                            grad_r.at[source],
                            y_mate,
                        ).wait_recv()
                total = grad_got[0, 1 - y].astype(f32)
                for k in range(1, depth):
                    total = total + grad_got[k, 1 - y].astype(f32)
                grad_y[...] = total.astype(bf16)
                send(role, send_grad_y)
            else:
                zt = real(last)
                for col in range(2):
                    if last != role or col == 1:
                        p = pair_of(last, col)
                        copy(
                            low_mine.at[p], low_got.at[p], low_s.at[p], low_r.at[p], p * 2 + c
                        ).wait_recv()
                both = low_got[pl.ds(zt * 2, 2)].reshape(2 * rank, 2 * tok)
                grads = adapter_scale * jnp.dot(
                    both, cots[...].reshape(2 * tok, width), preferred_element_type=f32
                )
                grads = grads.astype(bf16).reshape(2, rank, width)
                if last == role:
                    grad_got[zt] = grads
                else:
                    grad_mine[zt] = grads
                    send(role, lambda: send_grad(last))
        elif word == "back":
            both = cots[...].reshape(2 * tok, width)
            returned = transposed_dot(outs[...].reshape(pairs * rank, width), both)
            for p in range(pairs):
                weight = jnp.concatenate(
                    [kept[home * 2 + k, pl.ds(p * 2 + c, 1), :] for k in range(2)], axis=1
                )
                back_mine[p] = (returned[p * rank : (p + 1) * rank] * weight).astype(bf16)

            back_got[home] = back_mine[home]

            @pl.loop(0, pairs)
            def _(p):
                @pl.when(p != home)
                def _():
                    send_back(p).start()

        elif word == "gin":
            gin_ref[...] = jnp.zeros_like(gin_ref)

            @pl.loop(0, pairs)
            def _(p):
                @pl.when(p != home)
                def _():
                    copy(
                        back_mine.at[p], back_got.at[p], back_s.at[p], back_r.at[p], p * 2 + c
                    ).wait_recv()

                gin_ref[...] += adapter_scale * jnp.dot(
                    back_got[p], hid[p], preferred_element_type=f32
                )

        elif word == "gout":
            send_grad_y().wait_recv()
            total = grad_yin[...].astype(f32)
            for k in range(depth):
                total = total + grad_got[k, y].astype(f32)
            gout_ref[...] = total
        else:
            raise ValueError(name)

    waited = ([], [])
    plans = (OUTER, INNER)
    begin = [plan.index("kept") for plan in plans]
    computes = [[one for one in plan if one.startswith("pair")] for plan in plans]

    def steps(role, names):
        for name in names:
            step(role, name)

    def between(role, k):
        plan = plans[role]
        lo = begin[role] if k == 0 else plan.index(computes[role][k - 1])
        hi = plan.index(computes[role][k]) if k < pairs else len(plan)
        return plan[lo + 1 : hi]

    for role in range(2):
        pl.when(roles[role])(partial(steps, role, plans[role][: begin[role]]))
    find_kept()

    @pl.loop(0, pairs)
    def _(i):
        for k in range(pairs):
            for role in range(2):
                pl.when(roles[role] & (i == k))(partial(steps, role, between(role, k)))
        p = i * 0
        for role in range(2):
            for k in range(pairs):
                zz, col = (int(one) for one in computes[role][k][-2:])
                p = jnp.where(roles[role] & (i == k), pair_of(zz, col), p)
        tile_in(p).wait_recv()
        expert_pair(p)

    for role in range(2):
        pl.when(roles[role])(partial(steps, role, between(role, pairs)[:-1]))

    for level in range(levels):
        for one in send_near(level):
            one.wait_recv()
    near_in_ref[...] = near_in[...]
    near_out_ref[...] = near_out[...]

    @pl.loop(1, n)
    def _(d):
        send_table(d).wait_send()

    @pl.loop(0, pairs)
    def _(p):
        tile_to(p).wait_send()
        core_to(p).wait_send()

        @pl.when(p != home)
        def _():
            send_low(p).wait_send()
            send_back(p).wait_send()

    for level in range(levels):
        for one in send_near(level):
            one.wait_send()
    send_cot().wait_send()

    def finish(role):
        for make in started[role]:
            make().wait_send()
        step(role, plans[role][-1])

    for role in range(2):
        pl.when(roles[role])(partial(finish, role))


def layer(levels, cap, routes, weights, in_f, out_f, x, cot, gate, up, down):
    n = cap.shape[0]
    tok, width = cot.shape
    rank, units = in_f.shape
    pairs, depth = n // 2, n // 4
    vmem = pl.BlockSpec(memory_space=pltpu.VMEM)
    hbm = pl.BlockSpec(memory_space=pl.ANY)
    bf16 = jnp.bfloat16
    f32 = jnp.float32
    dma = pltpu.SemaphoreType.DMA
    main, side = tok - min(BACK_OUTER, BACK_INNER), max(BACK_OUTER, BACK_INNER)
    return pl.pallas_call(
        partial(layer_kernel, levels),
        out_shape=(
            pltpu.VMEM((tok, width), bf16),
            pltpu.VMEM((rank, units), f32),
            pltpu.VMEM((rank, width), f32),
            pltpu.VMEM((levels, rank, units), bf16),
            pltpu.VMEM((levels, rank, width), bf16),
        ),
        in_specs=[pl.BlockSpec(memory_space=pltpu.SMEM)] + [hbm] * 9,
        out_specs=(vmem,) * 5,
        scratch_shapes=[
            pltpu.VMEM((pairs, 2, tok, width), bf16),
            pltpu.VMEM((pairs, 2, tok, width), bf16),
            pltpu.VMEM((pairs, tok, width), bf16),
            pltpu.VMEM((depth, main, width), bf16),
            pltpu.VMEM((side, width), bf16),
            pltpu.VMEM((2, depth, main, width), bf16),
            pltpu.VMEM((2, pairs, side, width), bf16),
            pltpu.VMEM((pairs, 2 * tok, units), bf16),
            pltpu.VMEM((width, units), bf16),
            pltpu.VMEM((width, units), bf16),
            pltpu.VMEM((units, width), bf16),
            pltpu.VMEM((2, tok, width), bf16),
            pltpu.VMEM((rank, units), bf16),
            pltpu.VMEM((pairs, rank, width), bf16),
            pltpu.VMEM((n, n, tok), bf16),
            pltpu.VMEM((n, n, tok), f32),
            pltpu.VMEM((n, tok), f32),
            pltpu.VMEM((tok, n), f32),
            pltpu.VMEM((pairs, rank, 2 * tok), bf16),
            pltpu.VMEM((pairs, rank, 2 * tok), bf16),
            pltpu.VMEM((pairs, rank, 2 * tok), bf16),
            pltpu.VMEM((pairs, rank, 2 * tok), bf16),
            pltpu.VMEM((depth, 2, rank, width), bf16),
            pltpu.VMEM((depth, 2, rank, width), bf16),
            pltpu.VMEM((rank, width), bf16),
            pltpu.VMEM((rank, width), bf16),
            pltpu.VMEM((levels, rank, units), bf16),
            pltpu.VMEM((levels, rank, width), bf16),
            pltpu.VMEM(routes.shape, routes.dtype),
            pltpu.VMEM(weights.shape, weights.dtype),
            pltpu.VMEM(in_f.shape, f32),
            pltpu.VMEM(out_f.shape, f32),
            dma((3, depth, PARTS_OUT)),
            dma((pairs, PARTS_OUT)),
            dma((3, pairs)),
            dma((pairs,)),
            dma((3, pairs)),
            dma((pairs,)),
            dma((pairs,)),
            dma((pairs,)),
            dma((pairs,)),
            dma((pairs,)),
            dma((depth, PARTS_BACK)),
            dma((depth, PARTS_BACK)),
            dma((1,)),
            dma((1,)),
            dma((depth, PARTS_BACK)),
            dma((2, depth, PARTS_BACK)),
            dma((pairs,)),
            dma((2, pairs)),
            dma((n,)),
            dma((n,)),
            dma((pairs,)),
            dma((pairs,)),
            dma((pairs,)),
            dma((pairs,)),
            dma((depth,)),
            dma((depth,)),
            dma((1,)),
            dma((1,)),
            dma((1,)),
            dma((1,)),
            dma((2, levels)),
            dma((2, levels)),
            dma((9,)),
        ],
        compiler_params=pltpu.CompilerParams(
            collective_id=0, has_side_effects=True, vmem_limit_bytes=56 * 1024 * 1024
        ),
        cost_estimate=pl.CostEstimate(
            flops=20_000_000_000, bytes_accessed=30_000_000, transcendentals=0
        ),
    )(cap, routes, weights, in_f, out_f, x, cot, gate, up, down)


def adam_kernel(levels, level_ref, fix_one_ref, fix_two_ref, *refs):
    comb, near_in, near_out, grad_in, grad_out = refs[:5]
    given, made, done = refs[5:11], refs[11:18], refs[18]
    out = pltpu.make_async_copy(comb, made[0], done)
    out.start()
    fix_one, fix_two = fix_one_ref[0], fix_two_ref[0]
    for side in range(2):
        own, first, second = given[side * 3 : side * 3 + 3]
        new, new_first_ref, new_second_ref = made[1 + side], made[3 + side], made[5 + side]
        near = (near_in, near_out)[side]
        other = near[0].astype(jnp.float32)
        for level in range(1, levels):
            other = jnp.where(level_ref[0] == level, near[level].astype(jnp.float32), other)
        averaged = 0.5 * (own[...] + other)
        gradient = (grad_in, grad_out)[side][...]
        new_first = beta_one * first[...] + (1.0 - beta_one) * gradient
        new_second = beta_two * second[...] + (1.0 - beta_two) * gradient * gradient
        stepped = new_first / fix_one / (jnp.sqrt(new_second / fix_two) + epsilon)
        new[...] = averaged - learn_rate * (stepped + weight_decay * averaged)
        new_first_ref[...] = new_first
        new_second_ref[...] = new_second
    out.wait()


def adam(levels, level, fix_one, fix_two, *arrays):
    vmem = pl.BlockSpec(memory_space=pltpu.VMEM)
    smem = pl.BlockSpec(memory_space=pltpu.SMEM)
    hbm = pl.BlockSpec(memory_space=pl.ANY)
    comb, near_in, near_out, grad_in, grad_out = arrays[:5]
    f_in = jax.ShapeDtypeStruct(grad_in.shape, jnp.float32)
    f_out = jax.ShapeDtypeStruct(grad_out.shape, jnp.float32)
    return pl.pallas_call(
        partial(adam_kernel, levels),
        out_shape=(jax.ShapeDtypeStruct(comb.shape, comb.dtype), f_in, f_out, f_in, f_out, f_in, f_out),
        in_specs=[smem] * 3 + [vmem] * 11,
        out_specs=(hbm,) + (vmem,) * 6,
        scratch_shapes=[pltpu.SemaphoreType.DMA],
        compiler_params=pltpu.CompilerParams(vmem_limit_bytes=8 * 1024 * 1024),
    )(level, fix_one, fix_two, *arrays)


def per_device(
    tokens,
    cotangent,
    routes,
    router_pair_weight,
    capacity,
    training_step_index,
    frozen_gate_matrix,
    frozen_up_matrix,
    frozen_down_matrix,
    adapter_input_factor,
    adapter_output_factor,
    input_first_moment,
    output_first_moment,
    input_second_moment,
    output_second_moment,
):
    devices = lax.axis_size("exp")
    assert frozen_gate_matrix.shape[0] == 1 and devices == 16
    levels = lax.axis_size("rep").bit_length() - 1
    combined, grad_in, grad_out, near_in, near_out = layer(
        levels,
        capacity,
        routes[0].T,
        router_pair_weight[0].T,
        adapter_input_factor[0, 0],
        adapter_output_factor[0, 0],
        tokens[0],
        cotangent[0],
        frozen_gate_matrix[0],
        frozen_up_matrix[0],
        frozen_down_matrix[0],
    )
    level = training_step_index % levels
    power = (training_step_index + 1).astype(jnp.float32)
    fix_one = 1.0 - jnp.power(jnp.float32(beta_one), power)
    fix_two = 1.0 - jnp.power(jnp.float32(beta_two), power)
    results = adam(
        levels,
        level,
        fix_one,
        fix_two,
        combined,
        near_in,
        near_out,
        grad_in,
        grad_out,
        adapter_input_factor[0, 0],
        input_first_moment[0, 0],
        input_second_moment[0, 0],
        adapter_output_factor[0, 0],
        output_first_moment[0, 0],
        output_second_moment[0, 0],
    )
    return (results[0][None],) + tuple(one[None, None] for one in results[1:])


def solution(mesh):
    placed = (
        P("rep", "exp", None),
        P("rep", "exp", None),
        P("rep", "exp", None),
        P("rep", "exp", None),
        P(),
        P(),
        P("exp", None, None),
        P("exp", None, None),
        P("exp", None, None),
        P("rep", "exp", None, None),
        P("rep", "exp", None, None),
        P("rep", "exp", None, None),
        P("rep", "exp", None, None),
        P("rep", "exp", None, None),
        P("rep", "exp", None, None),
    )
    return jax.shard_map(
        per_device,
        mesh=mesh,
        in_specs=placed,
        out_specs=(
            P("rep", "exp", None),
            P("rep", "exp", None, None),
            P("rep", "exp", None, None),
            P("rep", "exp", None, None),
            P("rep", "exp", None, None),
            P("rep", "exp", None, None),
            P("rep", "exp", None, None),
        ),
        check_vma=False,
    )
```

```python
from functools import partial

import jax
import jax.numpy as jnp
from jax import lax
from jax.experimental import pallas as pl
from jax.experimental.pallas import tpu as pltpu
from jax.sharding import PartitionSpec as P

adapter_scale = 0.5
beta_one = 0.9
beta_two = 0.999
learn_rate = 0.02
weight_decay = 0.01
epsilon = 1e-08
MESH = pl.DeviceIdType.MESH
SIDE_OUT = 32
BACK_OUTER = 32
BACK_INNER = 48
PARTS_OUT = 2
PARTS_BACK = 2
OUTER = (
    "own", "fy10", "kept", "fy11", "fs1", "pair10", "fob0", "fsx1", "fsx0", "fy20", "ty1",
    "post10", "cs10", "pair11", "fy21", "fobx0", "fs2", "fm20", "post11", "ym11", "cs11", "fm11",
    "pair20", "fy30", "fsx2", "ty2", "post20", "cs20", "pair21", "ty0", "cm11", "fy31", "fm30",
    "fs3", "fm21", "ym10", "post21", "cs21", "ym20", "pair30", "fsx3", "ty3", "g11", "post30",
    "cs30", "pair31", "g12", "fob3", "post31", "ym31", "cs31", "ym30", "fob1", "g13", "pair01",
    "cm31", "cm30", "ym21", "pair00", "fob2", "post01", "cm20", "ym00", "g10", "back", "g2",
    "post00", "ym01", "fm31", "fm10", "cm21", "cm10", "gout", "ys", "gin", "fin2", "fin1",
)
INNER = (
    "own", "fsx1", "fm20", "kept", "fy21", "fm21", "fy20", "pair10", "ty1", "fm01", "fs2", "fy01",
    "fsx2", "fy00", "fm00", "fs0", "pair20", "ty2", "pair11", "fm30", "fsx0", "fy31", "fm31",
    "pair21", "fs3", "pair00", "fob0", "ty0", "fy30", "fob1", "g12", "fsx3", "post21", "pair30",
    "ty3", "ym20", "pair01", "post20", "fobx1", "cs20", "ym21", "fob3", "post11", "g11", "pair31",
    "fob2", "g13", "cs21", "back", "post31", "post01", "ym30", "ym00", "ym31", "post30", "g10",
    "cs30", "ym11", "post00", "ym01", "ys", "cs31", "post10", "cm31", "cs00", "g2", "ym10", "cs01",
    "cm30", "cm01", "cm20", "cm00", "cm21", "fin2", "gout", "gin", "fin1",
)


def cut_rows(rows, count, first=0):
    units = rows // 16
    ranges = []
    for one in range(count):
        size = 16 * (units // count + (1 if one < units % count else 0))
        ranges.append((first, first + size))
        first += size
    return ranges


def layer_kernel(
    levels,
    cap_ref,
    routes_hbm,
    weight_hbm,
    in_hbm,
    out_hbm,
    x_hbm,
    cot_hbm,
    gate_hbm,
    up_hbm,
    down_hbm,
    comb_ref,
    gin_ref,
    gout_ref,
    near_in_ref,
    near_out_ref,
    rows,
    part,
    from_core,
    from_y,
    from_ys,
    cm_in,
    cs_in,
    hid,
    gate_w,
    up_w,
    down_w,
    cots,
    in_b,
    outs,
    tables,
    kept,
    mine,
    mine_t,
    low_mine,
    low_got,
    back_mine,
    back_got,
    grad_mine,
    grad_got,
    grad_y,
    grad_yin,
    near_in,
    near_out,
    routes_ref,
    weight_ref,
    in_ref,
    out_ref,
    main_s,
    main_r,
    side_s,
    side_r,
    ob_s,
    ob_r,
    tile_s,
    tile_r,
    core_s,
    core_r,
    ym_s,
    ym_r,
    ys_s,
    ys_r,
    cm_s,
    cm_r,
    cs_s,
    cs_r,
    tab_s,
    tab_r,
    low_s,
    low_r,
    back_s,
    back_r,
    grad_s,
    grad_r,
    gy_s,
    gy_r,
    cot_s,
    cot_r,
    near_s,
    near_r,
    load_s,
):
    n = 16
    depth = 4
    pairs = n // 2
    f32 = jnp.float32
    bf16 = jnp.bfloat16
    me = lax.axis_index("exp")
    rep = lax.axis_index("rep")
    z, y, c = me // 4, (me // 2) % 2, me % 2
    home = me // 2
    tok = rows.shape[2]
    width = rows.shape[3]
    rank = outs.shape[1]
    cut_f = tok - SIDE_OUT
    out_parts = cut_rows(cut_f, PARTS_OUT)
    core_mate = me + 1 - 2 * c
    y_mate = me + 2 - 4 * y
    turned = z // 2
    sign = 1 - 2 * turned
    roles = ((z == 0) | (z == depth - 1), (z > 0) & (z < depth - 1))

    def real(zz):
        return 3 * turned + sign * zz

    def pair_of(zz, col):
        return real(zz) * 2 + (y if col == 0 else 1 - y)

    def cut_c(zz):
        return tok - (BACK_OUTER if zz in (0, depth - 1) else BACK_INNER)

    def back_parts(zz):
        return cut_rows(cut_c(zz), PARTS_BACK)

    def copy(src, dst, send, recv, device, axis="exp"):
        return pltpu.make_async_remote_copy(
            src_ref=src,
            dst_ref=dst,
            send_sem=send,
            recv_sem=recv,
            device_id={axis: device},
            device_id_type=MESH,
        )

    def towards(kind):
        return (me + 4 * sign, me - 4 * sign, y_mate)[kind]

    def moving(kind):
        return turned if kind == 0 else 1 - turned

    def main_to(kind, zz, part_at):
        lo, hi = out_parts[part_at]
        p = pair_of(zz, 0)
        block = rows.at[p, c, lo:hi]
        return copy(block, block, main_s.at[kind, zz, part_at], main_r.at[p, part_at], towards(kind))

    def main_in(zz, col, part_at):
        lo, hi = out_parts[part_at]
        p = pair_of(zz, col)
        block = rows.at[p, c, lo:hi]
        return copy(block, block, main_s.at[2, zz, part_at], main_r.at[p, part_at], y_mate)

    def side_to(kind, zz, col):
        p = pair_of(zz, col)
        block = rows.at[p, c, cut_f:tok]
        return copy(block, block, side_s.at[kind, zz * 2 + col], side_r.at[p], towards(kind))

    def ob_to(kind, zz, col):
        p = pair_of(zz, col)
        return copy(outs.at[p], outs.at[p], ob_s.at[kind, zz * 2 + col], ob_r.at[p], towards(kind))

    def tile_to(p):
        return copy(rows.at[p, c], rows.at[p, c], tile_s.at[p], tile_r.at[p], core_mate)

    def tile_in(p):
        return copy(rows.at[p, 1 - c], rows.at[p, 1 - c], tile_s.at[p], tile_r.at[p], core_mate)

    def core_to(p):
        return copy(part.at[p, 1 - c], from_core.at[p], core_s.at[p], core_r.at[p], core_mate)

    def ym_to(zz, part_at):
        lo, hi = back_parts(zz)[part_at]
        zt = real(zz)
        return copy(
            part.at[pair_of(zz, 1), c, lo:hi],
            from_y.at[zt, lo:hi],
            ym_s.at[zt, part_at],
            ym_r.at[zt, part_at],
            y_mate,
        )

    def ys_to(zz):
        size = tok - cut_c(zz)
        return copy(
            part.at[pair_of(zz, 1), c, cut_c(zz) : tok],
            from_ys.at[0:size],
            ys_s.at[0],
            ys_r.at[0],
            y_mate,
        )

    def cm_to(kind, zz, part_at):
        lo, hi = back_parts(zz)[part_at]
        zt = real(zz)
        return copy(
            part.at[pair_of(zz, 0), c, lo:hi],
            cm_in.at[moving(kind), zt, lo:hi],
            cm_s.at[zt, part_at],
            cm_r.at[moving(kind), zt, part_at],
            towards(kind),
        )

    def cs_to(kind, zz, col):
        p = pair_of(zz, col)
        size = tok - cut_c(zz)
        return copy(
            part.at[p, c, cut_c(zz) : tok],
            cs_in.at[moving(kind), p, 0:size],
            cs_s.at[p],
            cs_r.at[moving(kind), p],
            towards(kind),
        )

    def send_table(d):
        return copy(tables.at[me], tables.at[me], tab_s.at[d], tab_r.at[me], lax.rem(me + d, n))

    def send_low(p):
        return copy(low_mine.at[p], low_got.at[home], low_s.at[p], low_r.at[home], p * 2 + c)

    def send_back(p):
        return copy(back_mine.at[p], back_got.at[home], back_s.at[p], back_r.at[home], p * 2 + c)

    def send_grad(zz):
        zt = real(zz)
        return copy(grad_mine.at[zt], grad_got.at[z], grad_s.at[zt], grad_r.at[z], me + 4 * (zt - z))

    def send_grad_y():
        return copy(grad_y, grad_yin, gy_s.at[0], gy_r.at[0], y_mate)

    def send_cot():
        return copy(cots.at[c], cots.at[c], cot_s.at[0], cot_r.at[0], core_mate)

    def rep_mate(level):
        stride = 2**level
        return rep + stride * (1 - 2 * ((rep // stride) % 2))

    def send_near(level):
        return (
            copy(in_b, near_in.at[level], near_s.at[0, level], near_r.at[0, level], rep_mate(level), "rep"),
            copy(
                outs.at[home],
                near_out.at[level],
                near_s.at[1, level],
                near_r.at[1, level],
                rep_mate(level),
                "rep",
            ),
        )

    barrier = pltpu.get_barrier_semaphore()

    @pl.loop(1, n)
    def _(d):
        pl.semaphore_signal(
            barrier, inc=1, device_id={"exp": lax.rem(me + d, n)}, device_id_type=MESH
        )

    for level in range(levels):
        pl.semaphore_signal(
            barrier, inc=1, device_id={"rep": rep_mate(level)}, device_id_type=MESH
        )

    loads = [
        pltpu.make_async_copy(x_hbm, rows.at[home, c], load_s.at[0]),
        pltpu.make_async_copy(cot_hbm, cots.at[c], load_s.at[1]),
        pltpu.make_async_copy(gate_hbm, gate_w, load_s.at[2]),
        pltpu.make_async_copy(up_hbm, up_w, load_s.at[3]),
        pltpu.make_async_copy(down_hbm, down_w, load_s.at[4]),
    ]
    small = [
        pltpu.make_async_copy(source, target, load_s.at[5 + k])
        for k, (source, target) in enumerate(
            (
                (routes_hbm, routes_ref),
                (weight_hbm, weight_ref),
                (in_hbm, in_ref),
                (out_hbm, out_ref),
            )
        )
    ]
    for load in small + loads:
        load.start()
    for load in small:
        load.wait()

    in_b[...] = in_ref[...].astype(bf16)
    outs[home] = out_ref[...].astype(bf16)
    expert = lax.broadcasted_iota(jnp.int32, (n, tok), 0)
    routed = routes_ref[...]
    weights = weight_ref[...].astype(f32)
    table = jnp.zeros((n, tok), f32)
    for k in range(routes_ref.shape[0]):
        table = table + jnp.where(routed[k : k + 1] == expert, weights[k : k + 1], 0.0)
    tables[me] = table.astype(bf16)

    pl.semaphore_wait(barrier, n - 1 + levels)
    loads[0].wait()

    def transposed_dot(a, b):
        return lax.dot_general(a, b, (((1,), (1,)), ((), ())), preferred_element_type=f32)

    def find_kept():
        for level in range(levels):
            for one in send_near(level):
                one.start()
        loads[1].wait()
        send_cot().start()

        @pl.loop(1, n)
        def _(d):
            source = lax.rem(me + d, n)
            copy(
                tables.at[source], tables.at[source], tab_s.at[d], tab_r.at[source], source
            ).wait_recv()

        later = lax.broadcasted_iota(jnp.int32, (tok, tok), 1)
        sooner = lax.broadcasted_iota(jnp.int32, (tok, tok), 0)
        strictly = (sooner < later).astype(bf16)
        which_expert = lax.broadcasted_iota(jnp.int32, (n, 1), 0)
        cap = jnp.zeros((n, 1), f32)
        for e in range(n):
            cap = jnp.where(which_expert == e, cap_ref[e].astype(f32), cap)
        all_weights = tables[...].astype(f32).reshape(n * n, tok)
        hits = (all_weights > 0).astype(f32)
        within = jnp.dot(hits.astype(bf16), strictly, preferred_element_type=f32)
        counts = jnp.sum(hits, axis=1, keepdims=True)
        before = jnp.zeros((n, 1), f32)
        for source in range(n):
            part_of = slice(source * n, (source + 1) * n)
            keep = before + within[part_of] < cap
            row = jnp.where(keep, all_weights[part_of], 0.0)
            kept[source] = row
            mine[source : source + 1, :] = jnp.sum(
                jnp.where(expert == me, row, 0.0), axis=0, keepdims=True
            )
            before = before + counts[part_of]
        mine_t[...] = mine[...].T
        copy(cots.at[1 - c], cots.at[1 - c], cot_s.at[0], cot_r.at[0], core_mate).wait_recv()
        for load in loads[2:]:
            load.wait()

    lane = lax.broadcasted_iota(jnp.int32, (tok, n), 1)

    def expert_pair(p):
        x = rows[p].reshape(2 * tok, width)
        gate = jnp.dot(x, gate_w[...], preferred_element_type=f32)
        upper = jnp.dot(x, up_w[...], preferred_element_type=f32)
        hidden = (gate / (1.0 + jnp.exp(-gate)) * upper).astype(bf16)
        hid[p] = hidden
        low_t = transposed_dot(in_b[...], hidden).astype(bf16).astype(f32)
        low = transposed_dot(hidden, in_b[...]).astype(bf16)
        result = jnp.dot(hidden, down_w[...], preferred_element_type=f32)
        result = result + adapter_scale * jnp.dot(low, outs[home], preferred_element_type=f32)
        for k in range(2):
            scale = jnp.sum(jnp.where(lane == p * 2 + k, mine_t[...], 0.0), axis=1, keepdims=True)
            part[p, k] = (scale * result[k * tok : (k + 1) * tok]).astype(bf16)
        core_to(p).start()
        weighted = jnp.concatenate(
            [low_t[:, k * tok : (k + 1) * tok] * mine[pl.ds(p * 2 + k, 1), :] for k in range(2)],
            axis=1,
        ).astype(bf16)

        @pl.when(p == home)
        def _():
            low_got[p] = weighted

        @pl.when(p != home)
        def _():
            low_mine[p] = weighted
            send_low(p).start()

    started = ([], [])

    def send(role, make):
        make().start()
        started[role].append(make)

    def spread(role, zz, make):
        for kind, goes in ((0, zz <= role), (1, zz >= role and role > 0)):
            if goes:
                send(role, partial(make, kind))

    def sources(role):
        return ((1,), (0, 1))[role]

    def add_up(target, base, p, lo, hi, others):
        @pl.loop(0, (hi - lo) // 16)
        def _(k):
            at = pl.multiple_of(k * 16, 16)
            total = part[p, c, pl.ds(lo + at, 16)].astype(f32)
            for one in others:
                total = total + one[pl.ds(at, 16)].astype(f32)
            target[pl.ds(base + at, 16)] = total.astype(bf16)

    def add_part(p, lo, hi, others):
        add_up(part.at[p, c], lo, p, lo, hi, others)

    def arrived(role, zz, h):
        if (zz, h) not in waited[role]:
            waited[role].append((zz, h))
            main_in(zz, 0, h).wait_recv()

    def step(role, name):
        word = name.rstrip("0123456789")
        digits = [int(one) for one in name[len(word) :]]
        zz = digits[0] if digits else role
        last = digits[1] if len(digits) > 1 else 0
        along = 0 if zz > role else 1
        if word == "own":

            @pl.loop(1, n)
            def _(d):
                send_table(d).start()

            send(role, lambda: side_to(2, role, 0))
            for h in range(PARTS_OUT):
                spread(role, role, lambda kind, h=h: main_to(kind, role, h))
                send(role, lambda h=h: main_to(2, role, h))
            spread(role, role, lambda kind: side_to(kind, role, 0))
            tile_to(home).start()
        elif word == "fob":
            if zz == role:
                send(role, lambda: ob_to(2, role, 0))
                spread(role, role, lambda kind: ob_to(kind, role, 0))
            else:
                for col in range(2):
                    ob_to(2, zz, col).wait_recv()
                for col in range(2):
                    spread(role, zz, lambda kind, col=col: ob_to(kind, zz, col))
        elif word == "fobx":
            ob_to(2, role, 1).wait_recv()
            spread(role, role, lambda kind: ob_to(kind, role, 1))
        elif word in ("fm", "fy"):
            arrived(role, zz, last)
            if word == "fm":
                spread(role, zz, lambda kind: main_to(kind, zz, last))
            else:
                send(role, lambda: main_to(2, zz, last))
        elif word == "fs":
            for h in range(PARTS_OUT):
                arrived(role, zz, h)
            side_to(2, zz, 0).wait_recv()
            spread(role, zz, lambda kind: side_to(kind, zz, 0))
            tile_to(pair_of(zz, 0)).start()
        elif word == "fsx":
            side_to(2, zz, 1).wait_recv()
            spread(role, zz, lambda kind: side_to(kind, zz, 1))
        elif word == "ty":
            for h in range(PARTS_OUT):
                main_in(zz, 1, h).wait_recv()
            tile_to(pair_of(zz, 1)).start()
        elif word == "post":
            p = pair_of(zz, last)
            core_to(p).wait_recv()
            add_part(p, 0, tok, [from_core.at[p]])
        elif word == "ym":
            send(role, lambda: ym_to(zz, last))
        elif word == "cs":
            if role == 1:
                p = pair_of(zz, last)
                cs_to(along, zz, last).wait_recv()
                lo = cut_c(zz)
                add_part(p, lo, tok, [cs_in.at[moving(along), p]])
            send(role, lambda: cs_to(along, zz, last))
        elif word == "cm":
            p, zt = pair_of(zz, 0), real(zz)
            lo, hi = back_parts(zz)[last]
            ym_to(zz, last).wait_recv()
            others = [from_y.at[zt, lo:hi]]
            if role == 1:
                cm_to(along, zz, last).wait_recv()
                others.append(cm_in.at[moving(along), zt, lo:hi])
            add_part(p, lo, hi, others)
            send(role, lambda: cm_to(along, zz, last))
        elif word == "ys":
            p = pair_of(role, 1)
            lo = cut_c(role)
            for kind in sources(role):
                cs_to(kind, role, 1).wait_recv()
            add_part(p, lo, tok, [cs_in.at[moving(kind), p] for kind in sources(role)])
            send(role, lambda: ys_to(role))
        elif word == "fin":
            if name == "fin1":
                lo, hi = 0, cut_c(role)
                for h in range(PARTS_BACK):
                    ym_to(role, h).wait_recv()
                    for kind in sources(role):
                        cm_to(kind, role, h).wait_recv()
                others = [from_y.at[z, lo:hi]]
                others += [cm_in.at[moving(k), z, lo:hi] for k in sources(role)]
            else:
                lo, hi = cut_c(role), tok
                ys_to(role).wait_recv()
                for kind in sources(role):
                    cs_to(kind, role, 0).wait_recv()
                others = [from_ys] + [cs_in.at[moving(k), home] for k in sources(role)]
            add_up(comb_ref, lo, home, lo, hi, others)
        elif word == "g":
            if name == "g2":
                for k in range(depth):
                    if k != role:
                        source = real(k)
                        copy(
                            grad_mine.at[source],
                            grad_got.at[source],
                            grad_s.at[source],
                            grad_r.at[source],
                            y_mate,
                        ).wait_recv()
                total = grad_got[0, 1 - y].astype(f32)
                for k in range(1, depth):
                    total = total + grad_got[k, 1 - y].astype(f32)
                grad_y[...] = total.astype(bf16)
                send(role, send_grad_y)
            else:
                zt = real(last)
                for col in range(2):
                    if last != role or col == 1:
                        p = pair_of(last, col)
                        copy(
                            low_mine.at[p], low_got.at[p], low_s.at[p], low_r.at[p], p * 2 + c
                        ).wait_recv()
                both = low_got[pl.ds(zt * 2, 2)].reshape(2 * rank, 2 * tok)
                grads = adapter_scale * jnp.dot(
                    both, cots[...].reshape(2 * tok, width), preferred_element_type=f32
                )
                grads = grads.astype(bf16).reshape(2, rank, width)
                if last == role:
                    grad_got[zt] = grads
                else:
                    grad_mine[zt] = grads
                    send(role, lambda: send_grad(last))
        elif word == "back":
            both = cots[...].reshape(2 * tok, width)
            returned = transposed_dot(outs[...].reshape(pairs * rank, width), both)
            for p in range(pairs):
                weight = jnp.concatenate(
                    [kept[home * 2 + k, pl.ds(p * 2 + c, 1), :] for k in range(2)], axis=1
                )
                back_mine[p] = (returned[p * rank : (p + 1) * rank] * weight).astype(bf16)

            back_got[home] = back_mine[home]

            @pl.loop(0, pairs)
            def _(p):
                @pl.when(p != home)
                def _():
                    send_back(p).start()

        elif word == "gin":
            gin_ref[...] = jnp.zeros_like(gin_ref)

            @pl.loop(0, pairs)
            def _(p):
                @pl.when(p != home)
                def _():
                    copy(
                        back_mine.at[p], back_got.at[p], back_s.at[p], back_r.at[p], p * 2 + c
                    ).wait_recv()

                gin_ref[...] += adapter_scale * jnp.dot(
                    back_got[p], hid[p], preferred_element_type=f32
                )

        elif word == "gout":
            send_grad_y().wait_recv()
            total = grad_yin[...].astype(f32)
            for k in range(depth):
                total = total + grad_got[k, y].astype(f32)
            gout_ref[...] = total
        else:
            raise ValueError(name)

    waited = ([], [])
    plans = (OUTER, INNER)
    begin = [plan.index("kept") for plan in plans]
    computes = [[one for one in plan if one.startswith("pair")] for plan in plans]

    def steps(role, names):
        for name in names:
            step(role, name)

    def between(role, k):
        plan = plans[role]
        lo = begin[role] if k == 0 else plan.index(computes[role][k - 1])
        hi = plan.index(computes[role][k]) if k < pairs else len(plan)
        return plan[lo + 1 : hi]

    for role in range(2):
        pl.when(roles[role])(partial(steps, role, plans[role][: begin[role]]))
    find_kept()

    @pl.loop(0, pairs)
    def _(i):
        for k in range(pairs):
            for role in range(2):
                pl.when(roles[role] & (i == k))(partial(steps, role, between(role, k)))
        p = i * 0
        for role in range(2):
            for k in range(pairs):
                zz, col = (int(one) for one in computes[role][k][-2:])
                p = jnp.where(roles[role] & (i == k), pair_of(zz, col), p)
        tile_in(p).wait_recv()
        expert_pair(p)

    for role in range(2):
        pl.when(roles[role])(partial(steps, role, between(role, pairs)[:-1]))

    for level in range(levels):
        for one in send_near(level):
            one.wait_recv()
    near_in_ref[...] = near_in[...]
    near_out_ref[...] = near_out[...]

    @pl.loop(1, n)
    def _(d):
        send_table(d).wait_send()

    @pl.loop(0, pairs)
    def _(p):
        tile_to(p).wait_send()
        core_to(p).wait_send()

        @pl.when(p != home)
        def _():
            send_low(p).wait_send()
            send_back(p).wait_send()

    for level in range(levels):
        for one in send_near(level):
            one.wait_send()
    send_cot().wait_send()

    def finish(role):
        for make in started[role]:
            make().wait_send()
        step(role, plans[role][-1])

    for role in range(2):
        pl.when(roles[role])(partial(finish, role))


def layer(levels, cap, routes, weights, in_f, out_f, x, cot, gate, up, down):
    n = cap.shape[0]
    tok, width = cot.shape
    rank, units = in_f.shape
    pairs, depth = n // 2, n // 4
    vmem = pl.BlockSpec(memory_space=pltpu.VMEM)
    hbm = pl.BlockSpec(memory_space=pl.ANY)
    bf16 = jnp.bfloat16
    f32 = jnp.float32
    dma = pltpu.SemaphoreType.DMA
    main, side = tok - min(BACK_OUTER, BACK_INNER), max(BACK_OUTER, BACK_INNER)
    return pl.pallas_call(
        partial(layer_kernel, levels),
        out_shape=(
            pltpu.VMEM((tok, width), bf16),
            pltpu.VMEM((rank, units), f32),
            pltpu.VMEM((rank, width), f32),
            pltpu.VMEM((levels, rank, units), bf16),
            pltpu.VMEM((levels, rank, width), bf16),
        ),
        in_specs=[pl.BlockSpec(memory_space=pltpu.SMEM)] + [hbm] * 9,
        out_specs=(vmem,) * 5,
        scratch_shapes=[
            pltpu.VMEM((pairs, 2, tok, width), bf16),
            pltpu.VMEM((pairs, 2, tok, width), bf16),
            pltpu.VMEM((pairs, tok, width), bf16),
            pltpu.VMEM((depth, main, width), bf16),
            pltpu.VMEM((side, width), bf16),
            pltpu.VMEM((2, depth, main, width), bf16),
            pltpu.VMEM((2, pairs, side, width), bf16),
            pltpu.VMEM((pairs, 2 * tok, units), bf16),
            pltpu.VMEM((width, units), bf16),
            pltpu.VMEM((width, units), bf16),
            pltpu.VMEM((units, width), bf16),
            pltpu.VMEM((2, tok, width), bf16),
            pltpu.VMEM((rank, units), bf16),
            pltpu.VMEM((pairs, rank, width), bf16),
            pltpu.VMEM((n, n, tok), bf16),
            pltpu.VMEM((n, n, tok), f32),
            pltpu.VMEM((n, tok), f32),
            pltpu.VMEM((tok, n), f32),
            pltpu.VMEM((pairs, rank, 2 * tok), bf16),
            pltpu.VMEM((pairs, rank, 2 * tok), bf16),
            pltpu.VMEM((pairs, rank, 2 * tok), bf16),
            pltpu.VMEM((pairs, rank, 2 * tok), bf16),
            pltpu.VMEM((depth, 2, rank, width), bf16),
            pltpu.VMEM((depth, 2, rank, width), bf16),
            pltpu.VMEM((rank, width), bf16),
            pltpu.VMEM((rank, width), bf16),
            pltpu.VMEM((levels, rank, units), bf16),
            pltpu.VMEM((levels, rank, width), bf16),
            pltpu.VMEM(routes.shape, routes.dtype),
            pltpu.VMEM(weights.shape, weights.dtype),
            pltpu.VMEM(in_f.shape, f32),
            pltpu.VMEM(out_f.shape, f32),
            dma((3, depth, PARTS_OUT)),
            dma((pairs, PARTS_OUT)),
            dma((3, pairs)),
            dma((pairs,)),
            dma((3, pairs)),
            dma((pairs,)),
            dma((pairs,)),
            dma((pairs,)),
            dma((pairs,)),
            dma((pairs,)),
            dma((depth, PARTS_BACK)),
            dma((depth, PARTS_BACK)),
            dma((1,)),
            dma((1,)),
            dma((depth, PARTS_BACK)),
            dma((2, depth, PARTS_BACK)),
            dma((pairs,)),
            dma((2, pairs)),
            dma((n,)),
            dma((n,)),
            dma((pairs,)),
            dma((pairs,)),
            dma((pairs,)),
            dma((pairs,)),
            dma((depth,)),
            dma((depth,)),
            dma((1,)),
            dma((1,)),
            dma((1,)),
            dma((1,)),
            dma((2, levels)),
            dma((2, levels)),
            dma((9,)),
        ],
        compiler_params=pltpu.CompilerParams(
            collective_id=0, has_side_effects=True, vmem_limit_bytes=56 * 1024 * 1024
        ),
        cost_estimate=pl.CostEstimate(
            flops=20_000_000_000, bytes_accessed=30_000_000, transcendentals=0
        ),
    )(cap, routes, weights, in_f, out_f, x, cot, gate, up, down)


def adam_kernel(levels, level_ref, fix_one_ref, fix_two_ref, *refs):
    comb, near_in, near_out, grad_in, grad_out = refs[:5]
    given, made, done = refs[5:11], refs[11:18], refs[18]
    out = pltpu.make_async_copy(comb, made[0], done)
    out.start()
    fix_one, fix_two = fix_one_ref[0], fix_two_ref[0]
    for side in range(2):
        own, first, second = given[side * 3 : side * 3 + 3]
        new, new_first_ref, new_second_ref = made[1 + side], made[3 + side], made[5 + side]
        near = (near_in, near_out)[side]
        other = near[0].astype(jnp.float32)
        for level in range(1, levels):
            other = jnp.where(level_ref[0] == level, near[level].astype(jnp.float32), other)
        averaged = 0.5 * (own[...] + other)
        gradient = (grad_in, grad_out)[side][...]
        new_first = beta_one * first[...] + (1.0 - beta_one) * gradient
        new_second = beta_two * second[...] + (1.0 - beta_two) * gradient * gradient
        stepped = new_first / fix_one / (jnp.sqrt(new_second / fix_two) + epsilon)
        new[...] = averaged - learn_rate * (stepped + weight_decay * averaged)
        new_first_ref[...] = new_first
        new_second_ref[...] = new_second
    out.wait()


def adam(levels, level, fix_one, fix_two, *arrays):
    vmem = pl.BlockSpec(memory_space=pltpu.VMEM)
    smem = pl.BlockSpec(memory_space=pltpu.SMEM)
    hbm = pl.BlockSpec(memory_space=pl.ANY)
    comb, near_in, near_out, grad_in, grad_out = arrays[:5]
    f_in = jax.ShapeDtypeStruct(grad_in.shape, jnp.float32)
    f_out = jax.ShapeDtypeStruct(grad_out.shape, jnp.float32)
    return pl.pallas_call(
        partial(adam_kernel, levels),
        out_shape=(jax.ShapeDtypeStruct(comb.shape, comb.dtype), f_in, f_out, f_in, f_out, f_in, f_out),
        in_specs=[smem] * 3 + [vmem] * 11,
        out_specs=(hbm,) + (vmem,) * 6,
        scratch_shapes=[pltpu.SemaphoreType.DMA],
        compiler_params=pltpu.CompilerParams(vmem_limit_bytes=8 * 1024 * 1024),
    )(level, fix_one, fix_two, *arrays)


def per_device(
    tokens,
    cotangent,
    routes,
    router_pair_weight,
    capacity,
    training_step_index,
    frozen_gate_matrix,
    frozen_up_matrix,
    frozen_down_matrix,
    adapter_input_factor,
    adapter_output_factor,
    input_first_moment,
    output_first_moment,
    input_second_moment,
    output_second_moment,
):
    devices = lax.axis_size("exp")
    assert frozen_gate_matrix.shape[0] == 1 and devices == 16
    levels = lax.axis_size("rep").bit_length() - 1
    combined, grad_in, grad_out, near_in, near_out = layer(
        levels,
        capacity,
        routes[0].T,
        router_pair_weight[0].T,
        adapter_input_factor[0, 0],
        adapter_output_factor[0, 0],
        tokens[0],
        cotangent[0],
        frozen_gate_matrix[0],
        frozen_up_matrix[0],
        frozen_down_matrix[0],
    )
    level = training_step_index % levels
    power = (training_step_index + 1).astype(jnp.float32)
    fix_one = 1.0 - jnp.power(jnp.float32(beta_one), power)
    fix_two = 1.0 - jnp.power(jnp.float32(beta_two), power)
    results = adam(
        levels,
        level,
        fix_one,
        fix_two,
        combined,
        near_in,
        near_out,
        grad_in,
        grad_out,
        adapter_input_factor[0, 0],
        input_first_moment[0, 0],
        input_second_moment[0, 0],
        adapter_output_factor[0, 0],
        output_first_moment[0, 0],
        output_second_moment[0, 0],
    )
    return (results[0][None],) + tuple(one[None, None] for one in results[1:])


def solution(mesh):
    placed = (
        P("rep", "exp", None),
        P("rep", "exp", None),
        P("rep", "exp", None),
        P("rep", "exp", None),
        P(),
        P(),
        P("exp", None, None),
        P("exp", None, None),
        P("exp", None, None),
        P("rep", "exp", None, None),
        P("rep", "exp", None, None),
        P("rep", "exp", None, None),
        P("rep", "exp", None, None),
        P("rep", "exp", None, None),
        P("rep", "exp", None, None),
    )
    return jax.shard_map(
        per_device,
        mesh=mesh,
        in_specs=placed,
        out_specs=(
            P("rep", "exp", None),
            P("rep", "exp", None, None),
            P("rep", "exp", None, None),
            P("rep", "exp", None, None),
            P("rep", "exp", None, None),
            P("rep", "exp", None, None),
            P("rep", "exp", None, None),
        ),
        check_vma=False,
    )
```
